128 devices in a mesh: sys: 8 (over z_hi, x), edge: 16 (over y, z_lo, core).
Axes of the slice: x: 4, y: 4, z: 4 (z_hi: 2, z_lo: 2; z = z_hi * 2 + z_lo), core: 2. Of those that a mesh axis runs over, the one named last changes fastest.
Arguments:
- atoms: bfloat16 [8, 1024, 896], P('sys', 'edge'), may hold values from -6 to 6
- cotangent: bfloat16 [8, 1024, 896], P('sys', 'edge'), may hold values from -6 to 6
- experts: bfloat16 [32, 1792, 896], P('sys', 'edge'), may hold values from -0.125 to 0.125
- radial: bfloat16 [8, 32768, 896], P('sys', 'edge'), may hold values from -6 to 6
- coef: float32 [8, 32], replicated, may hold values from 0.02 to 0.5
- source: int32 [8, 32768], P('sys', 'edge'), may hold values from 0 to 1023
- target: int32 [8, 32768], P('sys', 'edge'), may hold values from 0 to 1023
Outputs:
- node_out: bfloat16 [8, 1024, 896], P('sys', 'edge')
- atom_grad: float32 [8, 1024, 896], P('sys', 'edge')
- expert_grad: float32 [32, 1792, 896], P('sys', 'edge')
The draws below stay inside these ranges and needn't reach their ends.
All inputs are finite; a program needn't handle non-finite values.
Results may differ from the reference program's by a relative error of at most 0.018.
Values may be sent and summed in bfloat16 or wider, within the bound.
A program may use at most 128 MiB of HBM per device.

```python
import math
import jax
import jax.numpy as jnp
from jax import lax

D = 896
DIN = 1792
EXPERTS = 32
EDGES = 32768
ATOMS = 1024
SYSTEMS = 8


def place_ends(entries, own_key, low, high):
    longest = entries.shape.index(max(entries.shape))
    spots = []
    for shift in (0, 1):
        where = [jax.random.randint(jax.random.fold_in(own_key, axis), (), 0, length) for axis, length in enumerate(entries.shape)]
        where[longest] = (where[longest] + shift) % entries.shape[longest]
        spots.append(tuple(where))
    return entries.at[spots[0]].set(low).at[spots[1]].set(high)


def shard_levels(key, shape, pieces, low, largest):
    loudness = 1.0
    for position, blocks in pieces:
        heights = jax.random.uniform(jax.random.fold_in(jax.random.fold_in(key, 6), position), (blocks,), jnp.float32, low / len(pieces), largest / len(pieces))
        loudness = loudness * jnp.repeat(jnp.exp(heights), shape[position] // blocks).reshape((-1,) + (1,) * (len(shape) - 1 - position))
    return loudness


def gaussian(stream_key, extent, width, reach, split=(), held_as=jnp.bfloat16):
    entries = jax.random.normal(stream_key, extent, jnp.float32) * width
    if len(split) > 0:
        entries = shard_levels(stream_key, extent, split, -0.22, 0.18) * entries
    return jnp.clip(entries, min=-reach, max=reach).astype(held_as)


def setup_inputs(seed: int = 0) -> dict:
    seeds = jax.random.split(jax.random.key(seed), 8)
    return {
        "atoms": gaussian(seeds[0], (SYSTEMS, ATOMS, D), 1.0, 6.0, ((0, 8), (1, 16))),
        "cotangent": gaussian(seeds[1], (SYSTEMS, ATOMS, D), 1.0, 6.0, ((0, 8), (1, 16))),
        "experts": gaussian(seeds[2], (EXPERTS, DIN, D), DIN ** -0.5, 0.125, ((0, 8), (1, 16))),
        "radial": gaussian(seeds[3], (SYSTEMS, EDGES, D), 1.0, 6.0, ((0, 8), (1, 16))),
        "coef": jnp.clip(jnp.exp(jax.random.uniform(seeds[4], (SYSTEMS, EXPERTS), jnp.float32, math.log(0.02), math.log(0.5))), 0.02, 0.5),
        "source": place_ends(jax.random.randint(seeds[5], (SYSTEMS, EDGES), 0, ATOMS), jax.random.fold_in(seeds[5], 1), 0, ATOMS - 1).astype(jnp.int32),
        "target": place_ends(jax.random.randint(seeds[6], (SYSTEMS, EDGES), 0, ATOMS), jax.random.fold_in(seeds[6], 1), 0, ATOMS - 1).astype(jnp.int32),
    }


def reference(atoms, cotangent, experts, radial, coef, source, target):
    merged_all = jnp.einsum("se,erd->srd", coef.astype(jnp.float32), experts.astype(jnp.float32), precision=lax.Precision.HIGHEST).astype(jnp.bfloat16)
    node_list = []
    grad_list = []
    merged_grads = []
    for sysnum in range(SYSTEMS):
        merged = merged_all[sysnum]
        feats = atoms[sysnum]
        edge_in = jnp.concatenate([jnp.take(feats, source[sysnum], axis=0), jnp.take(feats, target[sysnum], axis=0)], axis=1)
        pre = jnp.dot(edge_in, merged, preferred_element_type=jnp.float32)
        radial_f = radial[sysnum].astype(jnp.float32)
        message = (jax.nn.silu(pre) * radial_f).astype(jnp.bfloat16)
        node_sum = jax.ops.segment_sum(message.astype(jnp.float32), target[sysnum], num_segments=ATOMS)
        node_list.append(node_sum.astype(jnp.bfloat16))
        edge_cot = jnp.take(cotangent[sysnum], target[sysnum], axis=0).astype(jnp.float32)
        sigma = jax.nn.sigmoid(pre)
        slope = sigma * (1.0 + pre * (1.0 - sigma))
        pre_grad = (edge_cot * radial_f * slope).astype(jnp.bfloat16)
        input_grad = lax.dot_general(pre_grad, merged, (((1,), (1,)), ((), ())), preferred_element_type=jnp.float32).astype(jnp.bfloat16)
        first = jax.ops.segment_sum(input_grad[:, :D].astype(jnp.float32), source[sysnum], num_segments=ATOMS)
        second = jax.ops.segment_sum(input_grad[:, D:].astype(jnp.float32), target[sysnum], num_segments=ATOMS)
        grad_list.append(first + second)
        merged_grads.append(lax.dot_general(edge_in, pre_grad, (((0,), (0,)), ((), ())), preferred_element_type=jnp.float32))
    stacked = jnp.stack(merged_grads)
    expert_grad = jnp.einsum("se,srd->erd", coef.astype(jnp.float32), stacked, precision=lax.Precision.HIGHEST)
    return jnp.stack(node_list), jnp.stack(grad_list), expert_grad
```

```python
import functools

import jax
import jax.numpy as jnp
from jax import lax
from jax.experimental import pallas as pl
from jax.experimental.pallas import tpu as pltpu
from jax.sharding import PartitionSpec as P

F32 = jnp.float32
BF16 = jnp.bfloat16
MESH = pl.DeviceIdType.MESH
NX, NY = 4, 4
SHIFTS = (2, 1, 3)
SYS_STEPS = tuple((dz, dx) for dx in (2, 1, 3, 0) for dz in (1, 0) if (dz, dx) != (0, 0))


def dot(a, b):
    return lax.dot_general(a, b, (((1,), (0,)), ((), ())), preferred_element_type=F32)


def dot_t(a, b):
    return lax.dot_general(a, b, (((1,), (1,)), ((), ())), preferred_element_type=F32)


def kernel(
    chunks,
    experts,
    coef,
    atoms,
    cot,
    radial_hbm,
    src_rows,
    tgt_rows,
    src_line,
    tgt_line,
    node_out,
    atom_grad,
    expert_grad,
    radial,
    at_all,
    ct_all,
    oh_src,
    oh_tgt,
    ot_src,
    ot_tgt,
    sel_atoms,
    proj,
    edge_vals,
    per_chunk,
    local_sem,
    send_sem,
    recv_sem,
):
    n_exp, rows, width = experts.shape
    own_atoms = atoms.shape[0]
    n_atoms = 16 * own_atoms
    n_edges = radial.shape[0]
    n_sys = 2 * NX
    sys_id = lax.axis_index("sys")
    edge_id = lax.axis_index("edge")
    zh, x = sys_id // NX, sys_id % NX
    y, zl, c = edge_id // 4, (edge_id // 2) % 2, edge_id % 2
    plane = y * 2 + zl

    def sys_peer(dz, dx):
        return (((zh + dz) % 2) * NX + (x + dx) % NX, edge_id)

    def y_peer(d):
        return (sys_id, ((y + d) % NY) * 4 + zl * 2 + c)

    z_peer = (sys_id, y * 4 + (1 - zl) * 2 + c)
    c_peer = (sys_id, y * 4 + zl * 2 + (1 - c))

    radial_copy = pltpu.make_async_copy(radial_hbm, radial, local_sem.at[0])
    radial_copy.start()

    barrier = pltpu.get_barrier_semaphore()
    peers = [sys_peer(dz, dx) for dz, dx in SYS_STEPS] + [y_peer(d) for d in SHIFTS] + [z_peer, c_peer]
    for p in peers:
        pl.semaphore_signal(barrier, inc=1, device_id=p, device_id_type=MESH)
    pl.semaphore_wait(barrier, len(peers))

    sent = []

    def send(src, dst, peer):
        i = len(sent)
        cp = pltpu.make_async_remote_copy(
            src_ref=src,
            dst_ref=dst,
            send_sem=send_sem.at[i],
            recv_sem=recv_sem.at[i],
            device_id=peer,
            device_id_type=MESH,
        )
        cp.start()
        sent.append(cp)
        return cp

    at_all[pl.ds(plane, 1), pl.ds(c, 1)] = atoms[...][None, None]
    ct_all[pl.ds(plane, 1), pl.ds(c, 1)] = cot[...][None, None]
    pairs = ((atoms, at_all), (cot, ct_all))
    a_z = [send(own, full.at[plane, c], z_peer) for own, full in pairs]
    a_y = [send(own, full.at[plane, c], y_peer(d)) for own, full in pairs for d in SHIFTS]

    e_recv = [None] * len(chunks)

    def expert_part(k):
        start, size = chunks[k]
        b = per_chunk[k]
        e_recv[k] = []
        for i, (dz, dx) in enumerate(SYS_STEPS + ((0, 0),)):
            to = ((zh + dz) % 2) * NX + (x + dx) % NX
            total = jnp.zeros((rows, size), F32)
            for e in range(n_exp):
                total += coef[to, sys_id * n_exp + e] * experts[e, :, start : start + size].astype(F32)
            b["epart"][i] = total.astype(BF16)
            if (dz, dx) != (0, 0):
                e_recv[k].append(send(b["epart"].at[i], b["erecv"].at[i], sys_peer(dz, dx)))

    m_z, m_y, m_f = ([None] * len(chunks) for _ in range(3))

    def merge(k):
        b = per_chunk[k]
        for cp in e_recv[k]:
            cp.wait_recv()
        total = b["epart"][n_sys - 1].astype(F32)
        for i in range(n_sys - 1):
            total += b["erecv"][i].astype(F32)
        b["merged"][pl.ds(plane, 1), pl.ds(c, 1)] = total.astype(BF16)[None, None]
        own = b["merged"].at[plane, c]
        m_z[k] = send(own, own, z_peer)
        m_y[k] = [send(own, own, y_peer(d)) for d in SHIFTS]

    def merge_forward(k):
        m_z[k].wait_recv()
        other = per_chunk[k]["merged"].at[y * 2 + 1 - zl, c]
        m_f[k] = [send(other, other, y_peer(d)) for d in SHIFTS]

    def merge_finish(k):
        for cp in m_y[k] + m_f[k]:
            cp.wait_recv()
        half = per_chunk[k]["merged"].at[:, c]
        send(half, half, c_peer).wait_recv()

    def one_hots():
        lane = lax.broadcasted_iota(jnp.int32, (128, 128), 1)

        def by_edge(j, _):
            at = pl.ds(pl.multiple_of(j * 128, 128), 128)
            for idx, out in ((src_rows, oh_src), (tgt_rows, oh_tgt)):
                col = jnp.broadcast_to(idx[pl.ds(j, 1), :], (128, 128)).T
                for a in range(n_atoms // 128):
                    out[at, a * 128 : (a + 1) * 128] = jnp.where(col == lane + a * 128, 1.0, 0.0).astype(BF16)
            return 0

        lax.fori_loop(0, n_edges // 128, by_edge, 0)
        sub = lax.broadcasted_iota(jnp.int32, (64, n_edges), 0)

        def by_atom(j, _):
            at = pl.ds(pl.multiple_of(j * 64, 64), 64)
            for idx, out in ((src_line, ot_src), (tgt_line, ot_tgt)):
                line = jnp.broadcast_to(idx[...], (64, n_edges)) - j * 64
                out[at, :] = jnp.where(line == sub, 1.0, 0.0).astype(BF16)
            return 0

        lax.fori_loop(0, n_atoms // 64, by_atom, 0)

    def select_atoms():
        first = (edge_id % 8) * rows
        i = lax.broadcasted_iota(jnp.int32, (128, width), 0)
        j = lax.broadcasted_iota(jnp.int32, (128, width), 1)
        pick = jnp.where((j == i + first) & (i < rows), 1.0, 0.0).astype(BF16)
        sel_atoms[...] = dot_t(pick, at_all[...].reshape(n_atoms, width)).astype(BF16)

    def edges(k):
        start, size = chunks[k]
        b = per_chunk[k]
        cols = slice(start, start + size)

        def project(t, _):
            at = pl.ds(pl.multiple_of(t * 256, 256), 256)
            a = at_all[pl.ds(t * 2, 2)].reshape(256, width)
            for h in range(2):
                w = b["merged"][4 * h : 4 * h + 4].reshape(width, size)
                proj[h, at, 0:size] = dot(a, w).astype(BF16)
            return 0

        lax.fori_loop(0, n_atoms // 256, project, 0)

        def pick(t, _):
            at = pl.ds(pl.multiple_of(t * 512, 512), 512)
            o_s, o_t = oh_src[at, :], oh_tgt[at, :]
            pre = dot(o_s, proj[0, :, 0:size]) + dot(o_t, proj[1, :, 0:size])
            edge_cot = dot(o_t, ct_all[:, :, :, cols].reshape(n_atoms, size))
            r = radial[at, cols].astype(F32)
            g = 1.0 / (1.0 + jnp.exp(-pre))
            edge_vals[at, 0:size] = (edge_cot * r * (g * (1.0 + pre * (1.0 - g)))).astype(BF16)
            edge_vals[at, size : 2 * size] = (pre * g * r).astype(BF16)
            return 0

        lax.fori_loop(0, n_edges // 512, pick, 0)

    c_recv = [None] * len(chunks)

    def sums(k):
        size = chunks[k][1]
        b = per_chunk[k]
        c_recv[k] = []
        for d in SHIFTS + (0,):
            yy = (y + d) % NY
            at = pl.ds(pl.multiple_of(yy * 256, 256), 256)
            o_s, o_t = ot_src[at, :], ot_tgt[at, :]
            by_src = dot(o_s, edge_vals[:, 0:size]).astype(BF16)
            by_tgt = dot(o_t, edge_vals[:, 0 : 2 * size]).astype(BF16)
            for q in range(4):
                spot = (pl.ds(q % 2, 1), pl.ds(yy, 1), pl.ds(q // 2, 1))
                r = slice(q * own_atoms, (q + 1) * own_atoms)
                b["sums"][(*spot, slice(None), slice(0, size))] = by_src[r][None, None, None]
                b["sums"][(*spot, slice(None), slice(size, 3 * size))] = by_tgt[r][None, None, None]
            c_recv[k].append((d, send(b["sums"].at[1 - c, yy], b["csums"].at[yy], c_peer)))

    g_z, n_y, g_y, n_z, q_y, q_z, q_c, d_s = ([None] * len(chunks) for _ in range(8))

    def reduce_core(k):
        size = chunks[k][1]
        b = per_chunk[k]
        for d, cp in c_recv[k]:
            cp.wait_recv()
            yy = pl.ds((y + d) % NY, 1)
            both = b["sums"][pl.ds(c, 1), yy][0].astype(F32) + b["csums"][yy].astype(F32)
            b["chip"][yy] = both.astype(BF16)
        g_z[k] = send(b["chip"].at[:, 1 - zl, :, 0 : 2 * size], b["gz"], z_peer)
        n_y[k] = [
            send(b["chip"].at[(y + d) % NY, :, :, 2 * size : 3 * size], b["ny"].at[i], y_peer(d))
            for i, d in enumerate(SHIFTS)
        ]

    def reduce_z(k):
        size = chunks[k][1]
        b = per_chunk[k]
        g_z[k].wait_recv()
        own = b["chip"][:, pl.ds(zl, 1), :, 0 : 2 * size].reshape(NY, own_atoms, 2 * size)
        b["gsum"][...] = (own.astype(F32) + b["gz"][...].astype(F32)).astype(BF16)
        g_y[k] = [
            send(b["gsum"].at[(y + d) % NY], b["gy"].at[i], y_peer(d)) for i, d in enumerate(SHIFTS)
        ]

    def reduce_y(k):
        start, size = chunks[k]
        b = per_chunk[k]
        for cp in g_y[k]:
            cp.wait_recv()
        total = b["gsum"][pl.ds(y, 1)][0].astype(F32)
        for i in range(3):
            total += b["gy"][i].astype(F32)
        g = total.astype(BF16)
        b["gown"][0] = g[:, 0:size]
        b["gown"][1] = g[:, size : 2 * size]
        b["gall"][pl.ds(y, 1), pl.ds(zl, 1), pl.ds(c, 1)] = b["gown"][pl.ds(y // 2, 1)][None, None]
        q_y[k] = [
            send(b["gown"].at[((y + d) % NY) // 2], b["gall"].at[y, zl, c], y_peer(d)) for d in SHIFTS
        ]
        grad = dot_t(g[:, 0:size], b["merged"][0:4].reshape(width, size))
        grad += dot_t(g[:, size : 2 * size], b["merged"][4:8].reshape(width, size))
        if k == 0:
            atom_grad[...] = grad
        else:
            atom_grad[...] += grad

    def node_z(k):
        size = chunks[k][1]
        b = per_chunk[k]
        for cp in n_y[k]:
            cp.wait_recv()
        total = b["chip"][pl.ds(y, 1), :, :, 2 * size : 3 * size][0].astype(F32)
        for i in range(3):
            total += b["ny"][i].astype(F32)
        b["nsum"][...] = total.astype(BF16)
        n_z[k] = send(b["nsum"].at[1 - zl], b["nz"], z_peer)

    def node_finish(k):
        start, size = chunks[k]
        b = per_chunk[k]
        n_z[k].wait_recv()
        total = b["nsum"][pl.ds(zl, 1)][0].astype(F32) + b["nz"][...].astype(F32)
        node_out[:, start : start + size] = total.astype(BF16)

    def share_z(k):
        for cp in q_y[k]:
            cp.wait_recv()
        part = per_chunk[k]["gall"].at[:, zl, c]
        q_z[k] = send(part, part, z_peer)

    def share_c(k):
        q_z[k].wait_recv()
        part = per_chunk[k]["gall"].at[:, :, c]
        q_c[k] = send(part, part, c_peer)

    def weight_grad(k):
        size = chunks[k][1]
        b = per_chunk[k]
        q_c[k].wait_recv()
        grad = dot(sel_atoms[...], b["gall"][...].reshape(n_atoms, size))
        b["dall"][pl.ds(sys_id, 1)] = grad[0:rows].astype(BF16)[None]
        own = b["dall"].at[sys_id]
        d_s[k] = [send(own, own, sys_peer(dz, dx)) for dz, dx in SYS_STEPS]

    def expert_finish(k):
        start, size = chunks[k]
        b = per_chunk[k]
        for cp in d_s[k]:
            cp.wait_recv()
        for e in range(n_exp):
            total = jnp.zeros((rows, size), F32)
            for s in range(n_sys):
                total += coef[s, sys_id * n_exp + e] * b["dall"][s].astype(F32)
            expert_grad[e, :, start : start + size] = total

    n = len(chunks)
    for k in range(n):
        expert_part(k)
    one_hots()
    for cp in a_z:
        cp.wait_recv()
    other = y * 2 + 1 - zl
    a_f = [send(full.at[other, c], full.at[other, c], y_peer(d)) for _, full in pairs for d in SHIFTS]
    merge(0)
    merge_forward(0)
    for cp in a_y + a_f:
        cp.wait_recv()
    a_c = [send(full.at[:, c], full.at[:, c], c_peer) for _, full in pairs]
    if n > 1:
        merge(1)
    for cp in a_c:
        cp.wait_recv()
    select_atoms()
    radial_copy.wait()
    if n > 1:
        merge_forward(1)
    merge_finish(0)

    def steps(k, half):
        if half == 0:
            todo = [(merge, k + 2), (reduce_z, k - 1), (share_z, k - 2), (expert_finish, k - 3)]
        else:
            todo = [
                (reduce_core, k),
                (merge_forward, k + 2),
                (merge_finish, k + 1),
                (reduce_y, k - 1),
                (node_z, k - 1),
                (share_c, k - 2),
                (weight_grad, k - 2),
                (node_finish, k - 2),
            ]
        for f, i in todo:
            if 0 <= i < n:
                f(i)

    for k in range(n + 3):
        if k < n:
            edges(k)
        steps(k, 0)
        if k < n:
            sums(k)
        steps(k, 1)
    for cp in sent:
        cp.wait_send()


def layer(atoms, cotangent, experts, radial, coef, source, target):
    n_exp, rows, width = experts.shape
    own = atoms.shape[1]
    n_atoms = 16 * own
    n_edges = radial.shape[1]
    chunks, at = [], 0
    while at < width:
        size = min(256, width - at)
        chunks.append((at, size))
        at += size

    def vmem(*shape):
        return pltpu.VMEM(shape, BF16)

    per_chunk = [
        {
            "epart": vmem(8, rows, s),
            "erecv": vmem(8, rows, s),
            "merged": vmem(8, 2, rows, s),
            "sums": vmem(2, NY, 2, own, 3 * s),
            "csums": vmem(NY, 2, own, 3 * s),
            "chip": vmem(NY, 2, own, 3 * s),
            "gz": vmem(NY, own, 2 * s),
            "gsum": vmem(NY, own, 2 * s),
            "gy": vmem(3, own, 2 * s),
            "ny": vmem(3, 2, own, s),
            "nsum": vmem(2, own, s),
            "nz": vmem(own, s),
            "gown": vmem(2, own, s),
            "gall": vmem(NY, 2, 2, own, s),
            "dall": vmem(8, rows, s),
        }
        for _, s in chunks
    ]
    copies = 16 + 44 * len(chunks)
    wide = max(s for _, s in chunks)
    whole = pl.BlockSpec(memory_space=pltpu.VMEM)
    node, agrad, egrad = pl.pallas_call(
        functools.partial(kernel, chunks),
        out_shape=(
            jax.ShapeDtypeStruct((own, width), BF16),
            jax.ShapeDtypeStruct((own, width), F32),
            jax.ShapeDtypeStruct((n_exp, rows, width), F32),
        ),
        in_specs=[
            whole,
            pl.BlockSpec(memory_space=pltpu.SMEM),
            whole,
            whole,
            pl.BlockSpec(memory_space=pl.ANY),
            whole,
            whole,
            whole,
            whole,
        ],
        out_specs=(whole, whole, whole),
        scratch_shapes=[
            vmem(n_edges, width),
            vmem(8, 2, own, width),
            vmem(8, 2, own, width),
            vmem(n_edges, n_atoms),
            vmem(n_edges, n_atoms),
            vmem(n_atoms, n_edges),
            vmem(n_atoms, n_edges),
            vmem(128, n_atoms),
            vmem(2, n_atoms, wide),
            vmem(n_edges, 2 * wide),
            per_chunk,
            pltpu.SemaphoreType.DMA((1,)),
            pltpu.SemaphoreType.DMA((copies,)),
            pltpu.SemaphoreType.DMA((copies,)),
        ],
        compiler_params=pltpu.CompilerParams(
            collective_id=0, has_side_effects=True, vmem_limit_bytes=67043328
        ),
    )(
        experts,
        coef,
        atoms[0],
        cotangent[0],
        radial[0],
        source.reshape(n_edges // 128, 128),
        target.reshape(n_edges // 128, 128),
        source,
        target,
    )
    return node[None], agrad[None], egrad


def solution(mesh):
    spec = P("sys", "edge", None)
    return jax.shard_map(
        layer,
        mesh=mesh,
        in_specs=(spec, spec, spec, spec, P(), P("sys", "edge"), P("sys", "edge")),
        out_specs=(spec, spec, spec),
        check_vma=False,
    )
```

```python
import functools

import jax
import jax.numpy as jnp
from jax import lax
from jax.experimental import pallas as pl
from jax.experimental.pallas import tpu as pltpu
from jax.sharding import PartitionSpec as P

F32 = jnp.float32
BF16 = jnp.bfloat16
MESH = pl.DeviceIdType.MESH
NX, NY = 4, 4
SHIFTS = (2, 1, 3)
SYS_STEPS = tuple((dz, dx) for dx in (2, 1, 3, 0) for dz in (1, 0) if (dz, dx) != (0, 0))
EDGE_STEPS = tuple((dy, dz) for dy in (2, 1, 3, 0) for dz in (1, 0) if (dy, dz) != (0, 0))


def dot(a, b):
    return lax.dot_general(a, b, (((1,), (0,)), ((), ())), preferred_element_type=F32)


def dot_t(a, b):
    return lax.dot_general(a, b, (((1,), (1,)), ((), ())), preferred_element_type=F32)


def kernel(
    chunks,
    experts_hbm,
    coef,
    atoms_hbm,
    cot_hbm,
    radial_hbm,
    src_rows,
    tgt_rows,
    src_line,
    tgt_line,
    node_out,
    atom_grad,
    expert_grad,
    experts,
    radial,
    at_all,
    oh_src,
    oh_tgt,
    ot_src,
    ot_tgt,
    sel_atoms,
    proj,
    edge_vals,
    per_chunk,
    local_sem,
    send_sem,
    recv_sem,
):
    n_exp, rows, width = experts.shape
    own_atoms = atoms_hbm.shape[0]
    n_atoms = 16 * own_atoms
    n_edges = radial.shape[0]
    n = len(chunks)
    last = n - 1
    sys_id = lax.axis_index("sys")
    edge_id = lax.axis_index("edge")
    zh, x = sys_id // NX, sys_id % NX
    y, zl, c = edge_id // 4, (edge_id // 2) % 2, edge_id % 2
    plane = y * 2 + zl

    def sys_peer(dz, dx):
        return (((zh + dz) % 2) * NX + (x + dx) % NX, edge_id)

    def edge_peer(dy, dz):
        return (sys_id, ((y + dy) % NY) * 4 + ((zl + dz) % 2) * 2 + c)

    def y_peer(d):
        return edge_peer(d, 0)

    z_peer = edge_peer(0, 1)
    c_peer = (sys_id, y * 4 + zl * 2 + (1 - c))

    inputs = []

    def fetch(src, dst):
        cp = pltpu.make_async_copy(src, dst, local_sem.at[len(inputs)])
        cp.start()
        inputs.append(cp)
        return cp

    atoms_in = fetch(atoms_hbm, at_all.at[plane, c])
    cot_in = [
        fetch(cot_hbm.at[:, start : start + size], per_chunk[k]["cots"].at[plane, c])
        for k, (start, size) in enumerate(chunks)
    ]
    experts_in = fetch(experts_hbm, experts)
    radial_in = fetch(radial_hbm, radial)

    barrier = pltpu.get_barrier_semaphore()
    peers = [sys_peer(dz, dx) for dz, dx in SYS_STEPS] + [edge_peer(dy, dz) for dy, dz in EDGE_STEPS] + [c_peer]
    for p in peers:
        pl.semaphore_signal(barrier, inc=1, device_id=p, device_id_type=MESH)
    pl.semaphore_wait(barrier, len(peers))

    sent = []

    def send(src, dst, peer):
        i = len(sent)
        cp = pltpu.make_async_remote_copy(
            src_ref=src,
            dst_ref=dst,
            send_sem=send_sem.at[i],
            recv_sem=recv_sem.at[i],
            device_id=peer,
            device_id_type=MESH,
        )
        cp.start()
        sent.append(cp)
        return cp

    def share(full):
        own = full.at[plane, c]
        return {"full": full, "z": send(own, own, z_peer), "y": [send(own, own, y_peer(d)) for d in SHIFTS]}

    def share_forward(m):
        m["z"].wait_recv()
        other = m["full"].at[y * 2 + 1 - zl, c]
        m["y"] += [send(other, other, y_peer(d)) for d in SHIFTS]

    def share_core(m):
        for cp in m["y"]:
            cp.wait_recv()
        half = m["full"].at[:, c]
        m["c"] = send(half, half, c_peer)

    def share_wait(m):
        m["c"].wait_recv()

    e_x, e_z, merged_at, cots_at = ([None] * n for _ in range(4))

    def expert_part(k):
        start, size = chunks[k]
        b = per_chunk[k]
        for i, dx in enumerate(SHIFTS + (0,)):
            for z in range(2):
                to = z * NX + (x + dx) % NX
                total = jnp.zeros((rows, size), F32)
                for e in range(n_exp):
                    total += coef[to, sys_id * n_exp + e] * experts[e, :, start : start + size].astype(F32)
                b["epart"][i, z] = total.astype(BF16)
        e_x[k] = [send(b["epart"].at[i], b["erecv"].at[i], sys_peer(0, dx)) for i, dx in enumerate(SHIFTS)]

    def expert_x(k):
        b = per_chunk[k]
        for cp in e_x[k]:
            cp.wait_recv()
        total = b["epart"][3].astype(F32)
        for i in range(3):
            total += b["erecv"][i].astype(F32)
        b["esum"][...] = total.astype(BF16)
        e_z[k] = send(b["esum"].at[1 - zh], b["ez"], sys_peer(1, 0))

    def merge(k):
        b = per_chunk[k]
        e_z[k].wait_recv()
        total = b["esum"][pl.ds(zh, 1)][0].astype(F32) + b["ez"][...].astype(F32)
        b["merged"][pl.ds(plane, 1), pl.ds(c, 1)] = total.astype(BF16)[None, None]
        merged_at[k] = share(b["merged"])
        if k > 0:
            cots_at[k] = share(b["cots"])

    def merge_forward(k):
        share_forward(merged_at[k])
        if k > 0:
            share_forward(cots_at[k])

    def merge_core(k):
        share_core(merged_at[k])
        if k > 0:
            share_core(cots_at[k])

    def merge_wait(k):
        share_wait(merged_at[k])
        share_wait(cots_at[k])

    def one_hots():
        lane = lax.broadcasted_iota(jnp.int32, (128, 128), 1)

        def by_edge(j, _):
            at = pl.ds(pl.multiple_of(j * 128, 128), 128)
            for idx, out in ((src_rows, oh_src), (tgt_rows, oh_tgt)):
                col = jnp.broadcast_to(idx[pl.ds(j, 1), :], (128, 128)).T
                for a in range(n_atoms // 128):
                    out[at, a * 128 : (a + 1) * 128] = jnp.where(col == lane + a * 128, 1.0, 0.0).astype(BF16)
            return 0

        lax.fori_loop(0, n_edges // 128, by_edge, 0)
        sub = lax.broadcasted_iota(jnp.int32, (64, n_edges), 0)

        def by_atom(j, _):
            at = pl.ds(pl.multiple_of(j * 64, 64), 64)
            for idx, out in ((src_line, ot_src), (tgt_line, ot_tgt)):
                line = jnp.broadcast_to(idx[...], (64, n_edges)) - j * 64
                out[at, :] = jnp.where(line == sub, 1.0, 0.0).astype(BF16)
            return 0

        lax.fori_loop(0, n_atoms // 64, by_atom, 0)

    def select_atoms():
        first = (edge_id % 8) * rows
        i = lax.broadcasted_iota(jnp.int32, (128, width), 0)
        j = lax.broadcasted_iota(jnp.int32, (128, width), 1)
        pick = jnp.where((j == i + first) & (i < rows), 1.0, 0.0).astype(BF16)
        sel_atoms[...] = dot_t(pick, at_all[...].reshape(n_atoms, width)).astype(BF16)

    def edges(k):
        start, size = chunks[k]
        b = per_chunk[k]
        cols = slice(start, start + size)

        def project(t, _):
            at = pl.ds(pl.multiple_of(t * 256, 256), 256)
            a = at_all[pl.ds(t * 2, 2)].reshape(256, width)
            for h in range(2):
                w = b["merged"][4 * h : 4 * h + 4].reshape(width, size)
                proj[h, at, 0:size] = dot(a, w).astype(BF16)
            return 0

        lax.fori_loop(0, n_atoms // 256, project, 0)

        def pick(t, _):
            at = pl.ds(pl.multiple_of(t * 512, 512), 512)
            o_s, o_t = oh_src[at, :], oh_tgt[at, :]
            pre = dot(o_s, proj[0, :, 0:size]) + dot(o_t, proj[1, :, 0:size])
            edge_cot = dot(o_t, b["cots"][...].reshape(n_atoms, size))
            r = radial[at, cols].astype(F32)
            g = 1.0 / (1.0 + jnp.exp(-pre))
            edge_vals[at, 0:size] = (edge_cot * r * (g * (1.0 + pre * (1.0 - g)))).astype(BF16)
            edge_vals[at, size : 2 * size] = (pre * g * r).astype(BF16)
            return 0

        lax.fori_loop(0, n_edges // 512, pick, 0)

    c_recv = [None] * n

    def sums(k):
        size = chunks[k][1]
        b = per_chunk[k]
        c_recv[k] = []
        for d in SHIFTS + (0,):
            yy = (y + d) % NY
            at = pl.ds(pl.multiple_of(yy * 256, 256), 256)
            o_s, o_t = ot_src[at, :], ot_tgt[at, :]
            by_src = dot(o_s, edge_vals[:, 0:size]).astype(BF16)
            by_tgt = dot(o_t, edge_vals[:, 0 : 2 * size]).astype(BF16)
            for q in range(4):
                spot = (pl.ds(q % 2, 1), pl.ds(yy, 1), pl.ds(q // 2, 1))
                r = slice(q * own_atoms, (q + 1) * own_atoms)
                b["sums"][(*spot, slice(None), slice(0, size))] = by_src[r][None, None, None]
                b["sums"][(*spot, slice(None), slice(size, 3 * size))] = by_tgt[r][None, None, None]
            c_recv[k].append((d, send(b["sums"].at[1 - c, yy], b["csums"].at[yy], c_peer)))

    g_z, n_y, g_y, n_z, q_y, q_z, q_c, d_z, d_x = ([None] * n for _ in range(9))

    def reduce_core(k):
        size = chunks[k][1]
        b = per_chunk[k]
        for d, cp in c_recv[k]:
            cp.wait_recv()
            yy = pl.ds((y + d) % NY, 1)
            both = b["sums"][pl.ds(c, 1), yy][0].astype(F32) + b["csums"][yy].astype(F32)
            b["chip"][yy] = both.astype(BF16)
        if k == last:
            g_y[k] = [
                send(b["chip"].at[(y + dy) % NY, (zl + dz) % 2, :, 0 : 2 * size], b["gd"].at[i], edge_peer(dy, dz))
                for i, (dy, dz) in enumerate(EDGE_STEPS)
            ]
        else:
            g_z[k] = send(b["chip"].at[:, 1 - zl, :, 0 : 2 * size], b["gz"], z_peer)
        n_y[k] = [
            send(b["chip"].at[(y + d) % NY, :, :, 2 * size : 3 * size], b["ny"].at[i], y_peer(d))
            for i, d in enumerate(SHIFTS)
        ]

    def reduce_z(k):
        if k == last:
            return
        size = chunks[k][1]
        b = per_chunk[k]
        g_z[k].wait_recv()
        own = b["chip"][:, pl.ds(zl, 1), :, 0 : 2 * size].reshape(NY, own_atoms, 2 * size)
        b["gsum"][...] = (own.astype(F32) + b["gz"][...].astype(F32)).astype(BF16)
        g_y[k] = [
            send(b["gsum"].at[(y + d) % NY], b["gd"].at[i], y_peer(d)) for i, d in enumerate(SHIFTS)
        ]

    def reduce_y(k):
        size = chunks[k][1]
        b = per_chunk[k]
        for cp in g_y[k]:
            cp.wait_recv()
        if k == last:
            total = b["chip"][pl.ds(y, 1), pl.ds(zl, 1), :, 0 : 2 * size][0, 0].astype(F32)
        else:
            total = b["gsum"][pl.ds(y, 1)][0].astype(F32)
        for i in range(len(g_y[k])):
            total += b["gd"][i].astype(F32)
        g = total.astype(BF16)
        b["gown"][0] = g[:, 0:size]
        b["gown"][1] = g[:, size : 2 * size]
        b["gall"][pl.ds(y, 1), pl.ds(zl, 1), pl.ds(c, 1)] = b["gown"][pl.ds(y // 2, 1)][None, None]
        steps = EDGE_STEPS if k == last else tuple((d, 0) for d in SHIFTS)
        q_y[k] = [
            send(b["gown"].at[((y + dy) % NY) // 2], b["gall"].at[y, zl, c], edge_peer(dy, dz)) for dy, dz in steps
        ]
        grad = dot_t(g[:, 0:size], b["merged"][0:4].reshape(width, size))
        grad += dot_t(g[:, size : 2 * size], b["merged"][4:8].reshape(width, size))
        if k == 0:
            atom_grad[...] = grad
        else:
            atom_grad[...] += grad

    def node_z(k):
        size = chunks[k][1]
        b = per_chunk[k]
        for cp in n_y[k]:
            cp.wait_recv()
        total = b["chip"][pl.ds(y, 1), :, :, 2 * size : 3 * size][0].astype(F32)
        for i in range(3):
            total += b["ny"][i].astype(F32)
        b["nsum"][...] = total.astype(BF16)
        n_z[k] = send(b["nsum"].at[1 - zl], b["nz"], z_peer)

    def node_finish(k):
        start, size = chunks[k]
        b = per_chunk[k]
        n_z[k].wait_recv()
        total = b["nsum"][pl.ds(zl, 1)][0].astype(F32) + b["nz"][...].astype(F32)
        node_out[:, start : start + size] = total.astype(BF16)

    def grad_z(k):
        if k == last:
            return
        for cp in q_y[k]:
            cp.wait_recv()
        part = per_chunk[k]["gall"].at[:, zl, c]
        q_z[k] = send(part, part, z_peer)

    def grad_core(k):
        for cp in q_y[k] if k == last else [q_z[k]]:
            cp.wait_recv()
        part = per_chunk[k]["gall"].at[:, :, c]
        q_c[k] = send(part, part, c_peer)

    def weight_grad(k):
        size = chunks[k][1]
        b = per_chunk[k]
        q_c[k].wait_recv()
        grad = dot(sel_atoms[...], b["gall"][...].reshape(n_atoms, size))
        b["dall"][pl.ds(sys_id, 1)] = grad[0:rows].astype(BF16)[None]
        own = b["dall"].at[sys_id]
        if k == last:
            d_x[k] = [send(own, own, sys_peer(dz, dx)) for dz, dx in SYS_STEPS]
        else:
            d_z[k] = send(own, own, sys_peer(1, 0))
            d_x[k] = [send(own, own, sys_peer(0, dx)) for dx in SHIFTS]

    def expert_forward(k):
        if k == last:
            return
        d_z[k].wait_recv()
        other = per_chunk[k]["dall"].at[(1 - zh) * NX + x]
        d_x[k] += [send(other, other, sys_peer(0, dx)) for dx in SHIFTS]

    def expert_finish(k):
        start, size = chunks[k]
        b = per_chunk[k]
        for cp in d_x[k]:
            cp.wait_recv()
        for e in range(n_exp):
            total = jnp.zeros((rows, size), F32)
            for s in range(2 * NX):
                total += coef[s, sys_id * n_exp + e] * b["dall"][s].astype(F32)
            expert_grad[e, :, start : start + size] = total

    atoms_in.wait()
    atoms_at = share(at_all)
    for cp in cot_in:
        cp.wait()
    cots_at[0] = share(per_chunk[0]["cots"])
    experts_in.wait()
    for k in range(n):
        expert_part(k)
    one_hots()
    share_forward(atoms_at)
    share_forward(cots_at[0])
    expert_x(0)
    merge(0)
    expert_x(1)
    merge_forward(0)
    share_core(atoms_at)
    share_core(cots_at[0])
    merge(1)
    merge_core(0)
    share_wait(atoms_at)
    select_atoms()
    radial_in.wait()
    expert_x(2)
    merge_forward(1)
    merge_wait(0)

    def run(todo):
        for f, i in todo:
            if 0 <= i < n:
                f(i)

    for k in range(n):
        edges(k)
        run(
            [
                (merge_core, k + 1),
                (merge, k + 2),
                (expert_x, k + 3),
                (reduce_z, k - 1),
                (grad_z, k - 2),
                (expert_forward, k - 3),
            ]
        )
        sums(k)
        run(
            [
                (reduce_core, k),
                (merge_forward, k + 2),
                (merge_wait, k + 1),
                (reduce_y, k - 1),
                (node_z, k - 1),
                (grad_core, k - 2),
                (weight_grad, k - 2),
                (node_finish, k - 2),
            ]
        )
    run(
        [
            (grad_z, n - 2),
            (reduce_y, n - 1),
            (expert_forward, n - 3),
            (grad_core, n - 2),
            (weight_grad, n - 2),
            (node_z, n - 1),
            (grad_core, n - 1),
            (weight_grad, n - 1),
            (expert_forward, n - 2),
        ]
    )
    run([(node_finish, n - 2), (node_finish, n - 1)] + [(expert_finish, k) for k in range(n)])
    for cp in sent:
        cp.wait_send()


def layer(atoms, cotangent, experts, radial, coef, source, target):
    n_exp, rows, width = experts.shape
    own = atoms.shape[1]
    n_atoms = 16 * own
    n_edges = radial.shape[1]
    chunks, at = [], 0
    while at < width:
        size = min(256, width - at)
        chunks.append((at, size))
        at += size

    def vmem(*shape):
        return pltpu.VMEM(shape, BF16)

    per_chunk = [
        {
            "epart": vmem(4, 2, rows, s),
            "erecv": vmem(3, 2, rows, s),
            "esum": vmem(2, rows, s),
            "ez": vmem(rows, s),
            "cots": vmem(8, 2, own, s),
            "merged": vmem(8, 2, rows, s),
            "sums": vmem(2, NY, 2, own, 3 * s),
            "csums": vmem(NY, 2, own, 3 * s),
            "chip": vmem(NY, 2, own, 3 * s),
            "gz": vmem(NY, own, 2 * s),
            "gsum": vmem(NY, own, 2 * s),
            "gd": vmem(7, own, 2 * s),
            "ny": vmem(3, 2, own, s),
            "nsum": vmem(2, own, s),
            "nz": vmem(own, s),
            "gown": vmem(2, own, s),
            "gall": vmem(NY, 2, 2, own, s),
            "dall": vmem(8, rows, s),
        }
        for _, s in chunks
    ]
    copies = 8 + 54 * len(chunks)
    wide = max(s for _, s in chunks)
    whole = pl.BlockSpec(memory_space=pltpu.VMEM)
    hbm = pl.BlockSpec(memory_space=pl.ANY)
    node, agrad, egrad = pl.pallas_call(
        functools.partial(kernel, chunks),
        out_shape=(
            jax.ShapeDtypeStruct((own, width), BF16),
            jax.ShapeDtypeStruct((own, width), F32),
            jax.ShapeDtypeStruct((n_exp, rows, width), F32),
        ),
        in_specs=[
            hbm,
            pl.BlockSpec(memory_space=pltpu.SMEM),
            hbm,
            hbm,
            hbm,
            whole,
            whole,
            whole,
            whole,
        ],
        out_specs=(whole, whole, whole),
        scratch_shapes=[
            vmem(n_exp, rows, width),
            vmem(n_edges, width),
            vmem(8, 2, own, width),
            vmem(n_edges, n_atoms),
            vmem(n_edges, n_atoms),
            vmem(n_atoms, n_edges),
            vmem(n_atoms, n_edges),
            vmem(128, n_atoms),
            vmem(2, n_atoms, wide),
            vmem(n_edges, 2 * wide),
            per_chunk,
            pltpu.SemaphoreType.DMA((3 + len(chunks),)),
            pltpu.SemaphoreType.DMA((copies,)),
            pltpu.SemaphoreType.DMA((copies,)),
        ],
        compiler_params=pltpu.CompilerParams(
            collective_id=0, has_side_effects=True, vmem_limit_bytes=67043328
        ),
    )(
        experts,
        coef,
        atoms[0],
        cotangent[0],
        radial[0],
        source.reshape(n_edges // 128, 128),
        target.reshape(n_edges // 128, 128),
        source,
        target,
    )
    return node[None], agrad[None], egrad


def solution(mesh):
    spec = P("sys", "edge", None)
    return jax.shard_map(
        layer,
        mesh=mesh,
        in_specs=(spec, spec, spec, spec, P(), P("sys", "edge"), P("sys", "edge")),
        out_specs=(spec, spec, spec),
        check_vma=False,
    )
```

```python
import functools

import jax
import jax.numpy as jnp
from jax import lax
from jax.experimental import pallas as pl
from jax.experimental.pallas import tpu as pltpu
from jax.sharding import PartitionSpec as P

F32 = jnp.float32
BF16 = jnp.bfloat16
MESH = pl.DeviceIdType.MESH
NX, NY = 4, 4
SHIFTS = (2, 1, 3)
SEND_SLOTS = 64
RECV_SLOTS = 200
SYS_STEPS = tuple((dz, dx) for dx in (2, 1, 3, 0) for dz in (1, 0) if (dz, dx) != (0, 0))
EDGE_STEPS = tuple((dy, dz) for dy in (2, 1, 3, 0) for dz in (1, 0) if (dy, dz) != (0, 0))


def dot(a, b):
    return lax.dot_general(a, b, (((1,), (0,)), ((), ())), preferred_element_type=F32)


def dot_t(a, b):
    return lax.dot_general(a, b, (((1,), (1,)), ((), ())), preferred_element_type=F32)


def kernel(
    chunks,
    experts_hbm,
    coef,
    atoms_hbm,
    cot_hbm,
    radial_hbm,
    src_rows,
    tgt_rows,
    src_line,
    tgt_line,
    node_hbm,
    atom_hbm,
    expert_hbm,
    node_out,
    atom_grad,
    expert_grad,
    atom_total,
    atom_send,
    atom_z,
    atom_d,
    experts,
    radial,
    at_all,
    oh_src,
    oh_tgt,
    ot_src,
    ot_tgt,
    sel_atoms,
    proj,
    edge_vals,
    per_chunk,
    local_sem,
    send_sem,
    recv_sem,
):
    n_exp, rows, width = experts.shape
    own_atoms = atoms_hbm.shape[0]
    n_atoms = 16 * own_atoms
    n_edges = radial.shape[0]
    n = len(chunks)
    direct = n - 2
    sys_id = lax.axis_index("sys")
    edge_id = lax.axis_index("edge")
    zh, x = sys_id // NX, sys_id % NX
    y, zl, c = edge_id // 4, (edge_id // 2) % 2, edge_id % 2

    def sys_peer(dz, dx):
        return (((zh + dz) % 2) * NX + (x + dx) % NX, edge_id)

    def edge_peer(dy, dz):
        return (sys_id, ((y + dy) % NY) * 4 + ((zl + dz) % 2) * 2 + c)

    def y_peer(d):
        return edge_peer(d, 0)

    z_peer = edge_peer(0, 1)
    c_peer = (sys_id, y * 4 + zl * 2 + (1 - c))

    inputs = []

    def fetch(src, dst):
        cp = pltpu.make_async_copy(src, dst, local_sem.at[len(inputs)])
        cp.start()
        inputs.append(cp)
        return cp

    atoms_in = fetch(atoms_hbm, at_all.at[y, zl, c])
    cot_in = [
        fetch(cot_hbm.at[:, start : start + size], per_chunk[k]["cots"].at[y, zl, c])
        for k, (start, size) in enumerate(chunks)
    ]
    experts_in = fetch(experts_hbm, experts)
    radial_in = fetch(radial_hbm, radial)

    barrier = pltpu.get_barrier_semaphore()
    peers = [sys_peer(dz, dx) for dz, dx in SYS_STEPS] + [edge_peer(dy, dz) for dy, dz in EDGE_STEPS] + [c_peer]
    for p in peers:
        pl.semaphore_signal(barrier, inc=1, device_id=p, device_id_type=MESH)
    pl.semaphore_wait(barrier, len(peers))

    sent = []

    def send(src, dst, peer):
        i = len(sent)
        if i >= SEND_SLOTS:
            sent[i - SEND_SLOTS].wait_send()
        cp = pltpu.make_async_remote_copy(
            src_ref=src,
            dst_ref=dst,
            send_sem=send_sem.at[i % SEND_SLOTS],
            recv_sem=recv_sem.at[i],
            device_id=peer,
            device_id_type=MESH,
        )
        cp.start()
        sent.append(cp)
        return cp

    def share(full, cut):
        lo = full.at[:, :, :, 0:cut]
        own = lo.at[y, zl, c]
        m = {"full": full, "lo": lo, "y": []}
        if cut < full.shape[3]:
            m["hi"] = full.at[:, :, :, cut : full.shape[3]]
            block = m["hi"].at[y, zl, c]
            m["yh"] = [send(block, block, y_peer(d)) for d in SHIFTS]
        m["z"] = send(own, own, z_peer)
        m["y"] += [send(own, own, y_peer(d)) for d in SHIFTS]
        return m

    def share_forward(m):
        m["z"].wait_recv()
        other = m["lo"].at[y, 1 - zl, c]
        m["y"] += [send(other, other, y_peer(d)) for d in SHIFTS]

    def share_across(m):
        for cp in m["yh"]:
            cp.wait_recv()
        column = m["hi"].at[:, zl, c]
        m["y"].append(send(column, column, z_peer))

    def share_core(m):
        for cp in m["y"]:
            cp.wait_recv()
        half = m["full"].at[:, :, c]
        m["c"] = send(half, half, c_peer)

    def share_wait(m):
        m["c"].wait_recv()

    e_x, e_z, merged_at, cots_at = ([None] * n for _ in range(4))

    def expert_part(k):
        start, size = chunks[k]
        b = per_chunk[k]
        for i, dx in enumerate(SHIFTS + (0,)):
            for z in range(2):
                to = z * NX + (x + dx) % NX
                total = jnp.zeros((rows, size), F32)
                for e in range(n_exp):
                    total += coef[to, sys_id * n_exp + e] * experts[e, :, start : start + size].astype(F32)
                b["epart"][i, z] = total.astype(BF16)
        if k == 0:
            e_z[0] = [
                send(b["epart"].at[(SHIFTS + (0,)).index(dx), (zh + dz) % 2], b["ez"].at[i], sys_peer(dz, dx))
                for i, (dz, dx) in enumerate(SYS_STEPS)
            ]
        else:
            e_x[k] = [send(b["epart"].at[i], b["erecv"].at[i], sys_peer(0, dx)) for i, dx in enumerate(SHIFTS)]

    def expert_x(k):
        b = per_chunk[k]
        for cp in e_x[k]:
            cp.wait_recv()
        total = b["epart"][3].astype(F32)
        for i in range(3):
            total += b["erecv"][i].astype(F32)
        b["esum"][...] = total.astype(BF16)
        e_z[k] = [send(b["esum"].at[1 - zh], b["ez"].at[0], sys_peer(1, 0))]

    def merge(k):
        b = per_chunk[k]
        for cp in e_z[k]:
            cp.wait_recv()
        own = b["epart"].at[3] if k == 0 else b["esum"]
        total = own[pl.ds(zh, 1)][0].astype(F32)
        for i in range(len(e_z[k])):
            total += b["ez"][i].astype(F32)
        b["merged"][pl.ds(y, 1), pl.ds(zl, 1), pl.ds(c, 1)] = total.astype(BF16)[None, None, None]
        merged_at[k] = share(b["merged"], 48 if k == 0 else rows)
        if k > 0:
            cots_at[k] = share(b["cots"], own_atoms)

    def merge_forward(k):
        share_forward(merged_at[k])
        if k > 0:
            share_forward(cots_at[k])

    def merge_core(k):
        share_core(merged_at[k])
        if k > 0:
            share_core(cots_at[k])

    def merge_wait(k):
        share_wait(merged_at[k])
        share_wait(cots_at[k])

    def one_hots():
        lane = lax.broadcasted_iota(jnp.int32, (128, 128), 1)

        def by_edge(j, _):
            at = pl.ds(pl.multiple_of(j * 128, 128), 128)
            for idx, out in ((src_rows, oh_src), (tgt_rows, oh_tgt)):
                col = jnp.broadcast_to(idx[pl.ds(j, 1), :], (128, 128)).T
                for a in range(n_atoms // 128):
                    out[at, a * 128 : (a + 1) * 128] = jnp.where(col == lane + a * 128, 1.0, 0.0).astype(BF16)
            return 0

        lax.fori_loop(0, n_edges // 128, by_edge, 0)
        sub = lax.broadcasted_iota(jnp.int32, (64, n_edges), 0)

        def by_atom(j, _):
            at = pl.ds(pl.multiple_of(j * 64, 64), 64)
            for idx, out in ((src_line, ot_src), (tgt_line, ot_tgt)):
                line = jnp.broadcast_to(idx[...], (64, n_edges)) - j * 64
                out[at, :] = jnp.where(line == sub, 1.0, 0.0).astype(BF16)
            return 0

        lax.fori_loop(0, n_atoms // 64, by_atom, 0)

    def select_atoms():
        count = 4 * rows
        i = lax.broadcasted_iota(jnp.int32, (count, width), 0)
        j = lax.broadcasted_iota(jnp.int32, (count, width), 1)
        pick = jnp.where(j == i + (i // rows + c) * rows, 1.0, 0.0).astype(BF16)
        sel_atoms[...] = dot_t(pick, at_all[...].reshape(n_atoms, width)).astype(BF16)

    def project(k):
        size = chunks[k][1]
        b = per_chunk[k]
        narrow = 2 * size <= proj.shape[2]

        def body(t, _):
            at = pl.ds(pl.multiple_of(t * 256, 256), 256)
            a = at_all[pl.ds(t, 1)].reshape(256, width)
            w = [b["merged"][2 * h : 2 * h + 2].reshape(width, size) for h in range(2)]
            if narrow:
                both = dot(a, jnp.concatenate(w, axis=1)).astype(BF16)
                proj[0, at, 0:size] = both[:, 0:size]
                proj[1, at, 0:size] = both[:, size : 2 * size]
                proj[1, at, size : 2 * size] = b["cots"][pl.ds(t, 1)].reshape(256, size)
            else:
                for h in range(2):
                    proj[h, at, 0:size] = dot(a, w[h]).astype(BF16)
            return 0

        lax.fori_loop(0, NY, body, 0)

    def pick(k, half):
        start, size = chunks[k]
        b = per_chunk[k]
        narrow = 2 * size <= proj.shape[2]
        count = n_edges // 1024

        def body(t, _):
            at = pl.ds(pl.multiple_of(t * 512, 512), 512)
            o_s, o_t = oh_src[at, :], oh_tgt[at, :]
            if narrow:
                by_tgt = dot(o_t, proj[1, :, 0 : 2 * size])
                edge_cot = by_tgt[:, size : 2 * size]
                pre = dot(o_s, proj[0, :, 0:size]) + by_tgt[:, 0:size]
            else:
                pre = dot(o_s, proj[0, :, 0:size]) + dot(o_t, proj[1, :, 0:size])
                edge_cot = dot(o_t, b["cots"][...].reshape(n_atoms, size))
            r = radial[at, start : start + size].astype(F32)
            g = 1.0 / (1.0 + jnp.exp(-pre))
            edge_vals[at, 0:size] = (edge_cot * r * (g * (1.0 + pre * (1.0 - g)))).astype(BF16)
            edge_vals[at, size : 2 * size] = (pre * g * r).astype(BF16)
            return 0

        lax.fori_loop(half * count, (half + 1) * count, body, 0)

    c_recv = [None] * n

    def sums(k, tiles):
        size = chunks[k][1]
        b = per_chunk[k]
        if c_recv[k] is None:
            c_recv[k] = []
        for d in tiles:
            yy = (y + d) % NY
            at = pl.ds(pl.multiple_of(yy * 256, 256), 256)
            o_s, o_t = ot_src[at, :], ot_tgt[at, :]
            by_src = dot(o_s, edge_vals[:, 0:size]).astype(BF16)
            by_tgt = dot(o_t, edge_vals[:, 0 : 2 * size]).astype(BF16)
            spot = pl.ds(yy, 1)
            b["sums"][spot, :, :, :, 0:size] = by_src.reshape(1, 2, 2, own_atoms, size)
            b["sums"][spot, :, :, :, size : 3 * size] = by_tgt.reshape(1, 2, 2, own_atoms, 2 * size)
            c_recv[k].append((d, send(b["sums"].at[yy], b["csums"].at[yy], c_peer)))

    w_z, w_y, g_z, g_y, n_y, n_z, d_z, d_x = ([None] * n for _ in range(8))
    a_yz = []

    def to_edge(block_of, landing):
        return [send(block_of(dy, dz), landing.at[i], edge_peer(dy, dz)) for i, (dy, dz) in enumerate(EDGE_STEPS)]

    def atoms_of(dy, dz):
        return (y + dy) % NY, (zl + dz) % 2

    def reduce_core(k):
        size = chunks[k][1]
        b = per_chunk[k]
        for d, cp in c_recv[k]:
            cp.wait_recv()
            spot = pl.ds((y + d) % NY, 1)
            both = b["sums"][spot, :, :, :, 0 : 2 * size].astype(F32) + b["csums"][spot, :, :, :, 0 : 2 * size].astype(F32)
            b["chip"][spot] = both.astype(BF16)
        grad = dot(sel_atoms[...], b["chip"][...].reshape(n_atoms, 2 * size)).astype(BF16)
        b["wpart"][0:2] = grad[:, 0:size].reshape(2, 2, rows, size)
        b["wpart"][2:4] = grad[:, size : 2 * size].reshape(2, 2, rows, size)
        if k >= direct:
            w_y[k] = to_edge(lambda dy, dz: b["wpart"].at[atoms_of(dy, dz)], b["wd"])
            if k < n - 1:
                g_z[k] = send(b["chip"].at[:, 1 - zl, c], b["gz"], z_peer)
        else:
            w_z[k] = send(b["wpart"].at[:, 1 - zl], b["wz"], z_peer)

    def node_core(k):
        size = chunks[k][1]
        b = per_chunk[k]
        spot = (slice(None), slice(None), pl.ds(c, 1), slice(None), slice(2 * size, 3 * size))
        both = b["sums"][spot].astype(F32) + b["csums"][spot].astype(F32)
        b["nchip"][...] = both.astype(BF16).reshape(NY, 2, own_atoms, size)
        n_y[k] = [send(b["nchip"].at[(y + d) % NY], b["ny"].at[i], y_peer(d)) for i, d in enumerate(SHIFTS)]

    def node_z(k):
        b = per_chunk[k]
        for cp in n_y[k]:
            cp.wait_recv()
        total = b["nchip"][pl.ds(y, 1)][0].astype(F32)
        for i in range(3):
            total += b["ny"][i].astype(F32)
        b["nsum"][...] = total.astype(BF16)
        n_z[k] = send(b["nsum"].at[1 - zl], b["nz"], z_peer)

    def node_finish(k):
        start, size = chunks[k]
        b = per_chunk[k]
        n_z[k].wait_recv()
        total = b["nsum"][pl.ds(zl, 1)][0].astype(F32) + b["nz"][...].astype(F32)
        node_out[:, start : start + size] = total.astype(BF16)

    def atom_part(k):
        size = chunks[k][1]
        b = per_chunk[k]
        g = b["chip"][:, :, pl.ds(c, 1)].reshape(n_atoms // 2, 2 * size)
        grad = dot_t(g[:, 0:size], b["merged"][0:2].reshape(width, size))
        grad += dot_t(g[:, size : 2 * size], b["merged"][2:4].reshape(width, size))
        grad = grad.reshape(NY, 2, own_atoms, width)
        if k == 0:
            atom_total[...] = grad
        else:
            atom_total[...] += grad
        if k == direct - 1:
            atom_send[...] = atom_total[...].astype(BF16)
            a_yz.extend(send(atom_send.at[(y + d) % NY], atom_d.at[i], y_peer(d)) for i, d in enumerate(SHIFTS))

    def atom_y():
        for cp in a_yz:
            cp.wait_recv()
        a_yz.clear()
        total = atom_total[pl.ds(y, 1)][0]
        for i in range(3):
            total += atom_d[i].astype(F32)
        atom_send[pl.ds(y, 1)] = total.astype(BF16)[None]
        a_yz.append(send(atom_send.at[y, 1 - zl], atom_z, z_peer))
        atom_total[pl.ds(y, 1)] = total[None]

    def atom_finish():
        a_yz.pop().wait_recv()
        atom_grad[...] = atom_total[pl.ds(y, 1), pl.ds(zl, 1)].reshape(own_atoms, width) + atom_z[...].astype(F32)

    def atom_direct(k):
        b = per_chunk[k]
        g_y[k] = to_edge(lambda dy, dz: b["chip"].at[(*atoms_of(dy, dz), c)], b["gd"])

    def atom_staged(k):
        size = chunks[k][1]
        b = per_chunk[k]
        g_z[k].wait_recv()
        own = b["chip"][:, pl.ds(zl, 1), pl.ds(c, 1)].reshape(NY, own_atoms, 2 * size)
        b["gsum"][...] = (own.astype(F32) + b["gz"][...].astype(F32)).astype(BF16)
        g_y[k] = [send(b["gsum"].at[(y + d) % NY], b["gd"].at[i], y_peer(d)) for i, d in enumerate(SHIFTS)]

    def atom_last(k):
        size = chunks[k][1]
        b = per_chunk[k]
        for cp in g_y[k]:
            cp.wait_recv()
        if k == n - 1:
            total = b["chip"][pl.ds(y, 1), pl.ds(zl, 1), pl.ds(c, 1)][0, 0, 0].astype(F32)
        else:
            total = b["gsum"][pl.ds(y, 1)][0].astype(F32)
        for i in range(len(g_y[k])):
            total += b["gd"][i].astype(F32)
        g = total.astype(BF16)
        grad = dot_t(g[:, 0:size], b["merged"][0:2].reshape(width, size))
        grad += dot_t(g[:, size : 2 * size], b["merged"][2:4].reshape(width, size))
        atom_grad[...] += grad

    def weight_z(k):
        size = chunks[k][1]
        b = per_chunk[k]
        w_z[k].wait_recv()
        own = b["wpart"][:, pl.ds(zl, 1)].reshape(NY, rows, size)
        b["wsum"][...] = (own.astype(F32) + b["wz"][...].astype(F32)).astype(BF16)
        w_y[k] = [send(b["wsum"].at[(y + d) % NY], b["wd"].at[i], y_peer(d)) for i, d in enumerate(SHIFTS)]

    def weight_finish(k):
        b = per_chunk[k]
        for cp in w_y[k]:
            cp.wait_recv()
        if k >= direct:
            total = b["wpart"][pl.ds(y, 1), pl.ds(zl, 1)][0].astype(F32)
        else:
            total = b["wsum"][pl.ds(y, 1)].astype(F32)
        for i in range(len(w_y[k])):
            total += b["wd"][i : i + 1].astype(F32)
        b["dall"][pl.ds(sys_id, 1)] = total.astype(BF16)
        own = b["dall"].at[sys_id]
        if k == n - 1:
            d_x[k] = [send(own, own, sys_peer(dz, dx)) for dz, dx in SYS_STEPS]
        else:
            d_z[k] = send(own, own, sys_peer(1, 0))
            d_x[k] = [send(own, own, sys_peer(0, dx)) for dx in SHIFTS]

    def expert_forward(k):
        d_z[k].wait_recv()
        other = per_chunk[k]["dall"].at[(1 - zh) * NX + x]
        d_x[k] += [send(other, other, sys_peer(0, dx)) for dx in SHIFTS]

    def expert_finish(k):
        start, size = chunks[k]
        b = per_chunk[k]
        for cp in d_x[k]:
            cp.wait_recv()
        for e in range(n_exp):
            total = jnp.zeros((rows, size), F32)
            for s in range(2 * NX):
                total += coef[s, sys_id * n_exp + e] * b["dall"][s].astype(F32)
            expert_grad[e, :, start : start + size] = total
        cols = slice(start, start + size)
        outputs.append(fetch(expert_grad.at[:, :, cols], expert_hbm.at[:, :, cols]))

    outputs = []
    atoms_in.wait()
    atoms_at = share(at_all, own_atoms // 2)
    for cp in cot_in:
        cp.wait()
    cots_at[0] = share(per_chunk[0]["cots"], own_atoms // 2)
    experts_in.wait()
    for k in range(n):
        expert_part(k)
    one_hots()
    share_forward(atoms_at)
    share_forward(cots_at[0])
    share_across(atoms_at)
    share_across(cots_at[0])
    merge(0)
    share_forward(merged_at[0])
    expert_x(1)
    share_core(atoms_at)
    share_across(merged_at[0])
    share_core(cots_at[0])
    share_wait(atoms_at)
    select_atoms()
    share_core(merged_at[0])
    radial_in.wait()
    merge_wait(0)

    work = (
        (project,),
        (lambda k: pick(k, 0),),
        (lambda k: pick(k, 1),),
        (lambda k: sums(k, SHIFTS[0:1]),),
        (lambda k: sums(k, SHIFTS[1:2]),),
        (lambda k: sums(k, SHIFTS[2:3]),),
        (lambda k: sums(k, (0,)),),
    )
    beside = {
        (0, 0): ((merge, 1), (expert_x, 2)),
        (0, 1): ((merge_forward, 1),),
        (0, 2): ((merge, 2),),
        (0, 4): ((merge_core, 1),),
        (0, 5): ((merge_forward, 2), (expert_x, 3)),
        (0, 6): ((merge_wait, 1),),
        (1, 0): ((reduce_core, 0), (node_core, 0), (atom_part, 0)),
        (1, 1): ((merge, 3),),
        (1, 2): ((merge_core, 2),),
        (1, 4): ((merge_wait, 2),),
        (1, 5): ((merge_forward, 3), (weight_z, 0)),
        (2, 0): ((reduce_core, 1), (node_core, 1), (atom_part, 1)),
        (2, 2): ((merge_core, 3), (weight_finish, 0)),
        (2, 3): ((node_z, 0),),
        (2, 4): ((merge_wait, 3),),
        (2, 5): ((weight_z, 1),),
        (2, 6): ((expert_forward, 0),),
        (3, 0): ((reduce_core, 2), (node_core, 2)),
        (3, 2): ((weight_finish, 1),),
        (3, 3): ((node_z, 1),),
    }
    for k in range(n):
        for slot, (f,) in enumerate(work):
            f(k)
            for g, i in beside.get((k, slot), ()):
                g(i)
            if (k, slot) == (3, 4):
                atom_y()
    reduce_core(3)
    node_core(3)
    expert_forward(1)
    weight_finish(2)
    atom_direct(3)
    atom_staged(2)
    expert_finish(0)
    weight_finish(3)
    expert_forward(2)
    atom_finish()
    expert_finish(1)
    atom_last(3)
    node_z(2)
    node_z(3)
    atom_last(2)
    outputs.append(fetch(atom_grad, atom_hbm))
    for k in range(n):
        node_finish(k)
    outputs.append(fetch(node_out, node_hbm))
    expert_finish(2)
    expert_finish(3)

    def finish():
        for cp in outputs:
            cp.wait()

    def drain():
        for cp in sent[-SEND_SLOTS:]:
            cp.wait_send()
        assert len(sent) == recv_sem.shape[0], len(sent)

    finish()
    drain()


def write_out(*refs):
    count = (len(refs) - 1) // 3
    sem = refs[-1]
    moves = []
    for src, dst, buf in zip(refs[:count], refs[count : 2 * count], refs[2 * count : 3 * count]):
        for i in range(src.shape[0]):
            moves.append((src.at[i], buf.at[i], dst.at[i]))
    reads = [pltpu.make_async_copy(s, b, sem.at[0, i]) for i, (s, b, _) in enumerate(moves)]
    writes = [pltpu.make_async_copy(b, d, sem.at[1, i]) for i, (_, b, d) in enumerate(moves)]
    for r in reads:
        r.start()
    for r, w in zip(reads, writes):
        r.wait()
        w.start()
    for w in writes:
        w.wait()


def layer(atoms, cotangent, experts, radial, coef, source, target):
    n_exp, rows, width = experts.shape
    own = atoms.shape[1]
    n_atoms = 16 * own
    n_edges = radial.shape[1]
    chunks, at = [], 0
    while at < width:
        size = min(256, width - at)
        chunks.append((at, size))
        at += size

    def vmem(*shape):
        return pltpu.VMEM(shape, BF16)

    per_chunk = [
        {
            "epart": vmem(4, 2, rows, s),
            "erecv": vmem(3, 2, rows, s),
            "esum": vmem(2, rows, s),
            "ez": vmem(7 if k == 0 else 1, rows, s),
            "cots": vmem(NY, 2, 2, own, s),
            "merged": vmem(NY, 2, 2, rows, s),
            "sums": vmem(NY, 2, 2, own, 3 * s),
            "csums": vmem(NY, 2, 2, own, 3 * s),
            "chip": vmem(NY, 2, 2, own, 2 * s),
            "nchip": vmem(NY, 2, own, s),
            "ny": vmem(3, 2, own, s),
            "nsum": vmem(2, own, s),
            "nz": vmem(own, s),
            "gz": vmem(NY if k == 2 else 1, own, 2 * s),
            "gsum": vmem(NY if k == 2 else 1, own, 2 * s),
            "gd": vmem(7 if k == 3 else 3, own, 2 * s),
            "wpart": vmem(NY, 2, rows, s),
            "wz": vmem(NY, rows, s),
            "wsum": vmem(NY, rows, s),
            "wd": vmem(7, rows, s),
            "dall": vmem(8, rows, s),
        }
        for k, (_, s) in enumerate(chunks)
    ]
    wide = max(s for _, s in chunks)
    whole = pl.BlockSpec(memory_space=pltpu.VMEM)
    hbm = pl.BlockSpec(memory_space=pl.ANY)
    node, agrad, egrad = pl.pallas_call(
        functools.partial(kernel, chunks),
        out_shape=(
            jax.ShapeDtypeStruct((own, width), BF16),
            jax.ShapeDtypeStruct((own, width), F32),
            jax.ShapeDtypeStruct((n_exp, rows, width), F32),
        ),
        in_specs=[
            hbm,
            pl.BlockSpec(memory_space=pltpu.SMEM),
            hbm,
            hbm,
            hbm,
            whole,
            whole,
            whole,
            whole,
        ],
        out_specs=(hbm, hbm, hbm),
        scratch_shapes=[
            vmem(own, width),
            pltpu.VMEM((own, width), F32),
            pltpu.VMEM((n_exp, rows, width), F32),
            pltpu.VMEM((NY, 2, own, width), F32),
            vmem(NY, 2, own, width),
            vmem(own, width),
            vmem(3, 2, own, width),
            vmem(n_exp, rows, width),
            vmem(n_edges, width),
            vmem(NY, 2, 2, own, width),
            vmem(n_edges, n_atoms),
            vmem(n_edges, n_atoms),
            vmem(n_atoms, n_edges),
            vmem(n_atoms, n_edges),
            vmem(4 * rows, n_atoms),
            vmem(2, n_atoms, wide),
            vmem(n_edges, 2 * wide),
            per_chunk,
            pltpu.SemaphoreType.DMA((5 + 2 * len(chunks),)),
            pltpu.SemaphoreType.DMA((SEND_SLOTS,)),
            pltpu.SemaphoreType.DMA((RECV_SLOTS,)),
        ],
        compiler_params=pltpu.CompilerParams(
            collective_id=0, has_side_effects=True, vmem_limit_bytes=67043328
        ),
    )(
        experts,
        coef,
        atoms[0],
        cotangent[0],
        radial[0],
        source.reshape(n_edges // 128, 128),
        target.reshape(n_edges // 128, 128),
        source,
        target,
    )
    results = (node[None], agrad[None], egrad)
    moves = sum(r.shape[0] for r in results)
    return pl.pallas_call(
        write_out,
        out_shape=tuple(jax.ShapeDtypeStruct(r.shape, r.dtype) for r in results),
        in_specs=[hbm] * 3,
        out_specs=(hbm,) * 3,
        scratch_shapes=[pltpu.VMEM(r.shape, r.dtype) for r in results] + [pltpu.SemaphoreType.DMA((2, moves))],
    )(*results)


def solution(mesh):
    spec = P("sys", "edge", None)
    return jax.shard_map(
        layer,
        mesh=mesh,
        in_specs=(spec, spec, spec, spec, P(), P("sys", "edge"), P("sys", "edge")),
        out_specs=(spec, spec, spec),
        check_vma=False,
    )
```

```python
import functools

import jax
import jax.numpy as jnp
from jax import lax
from jax.experimental import pallas as pl
from jax.experimental.pallas import tpu as pltpu
from jax.sharding import PartitionSpec as P

F32 = jnp.float32
BF16 = jnp.bfloat16
MESH = pl.DeviceIdType.MESH
NX, NY = 4, 4
SHIFTS = (2, 1, 3)
SEND_SLOTS = 40
Z_FIRST = (0, 2)
RECV_SLOTS = 88
SYS_STEPS = tuple((dz, dx) for dx in (2, 1, 3, 0) for dz in (1, 0) if (dz, dx) != (0, 0))
EDGE_STEPS = tuple((dy, dz) for dy in (2, 1, 3, 0) for dz in (1, 0) if (dy, dz) != (0, 0))


def dot(a, b):
    return lax.dot_general(a, b, (((1,), (0,)), ((), ())), preferred_element_type=F32)


def dot_t(a, b):
    return lax.dot_general(a, b, (((1,), (1,)), ((), ())), preferred_element_type=F32)


def kernel(
    chunks,
    experts_hbm,
    coef_hbm,
    atoms_hbm,
    cot_hbm,
    radial_hbm,
    src_rows_hbm,
    tgt_rows_hbm,
    src_line_hbm,
    tgt_line_hbm,
    node_hbm,
    atom_hbm,
    expert_hbm,
    node_out,
    atom_grad,
    expert_grad,
    coef,
    src_rows,
    tgt_rows,
    src_line,
    tgt_line,
    experts,
    radial,
    at_all,
    oh_src,
    oh_tgt,
    ot_src,
    ot_tgt,
    sel_atoms,
    proj,
    edge_vals,
    per_chunk,
    local_sem,
    send_sem,
    recv_sem,
):
    n_exp, rows, width = experts.shape
    own_atoms = atoms_hbm.shape[0]
    n_atoms = 16 * own_atoms
    n_edges = radial.shape[0]
    n = len(chunks)
    sys_id = lax.axis_index("sys")
    edge_id = lax.axis_index("edge")
    zh, x = sys_id // NX, sys_id % NX
    y, zl, c = edge_id // 4, (edge_id // 2) % 2, edge_id % 2

    def sys_peer(dz, dx):
        return (((zh + dz) % 2) * NX + (x + dx) % NX, edge_id)

    def edge_peer(dy, dz):
        return (sys_id, ((y + dy) % NY) * 4 + ((zl + dz) % 2) * 2 + c)

    def y_peer(d):
        return edge_peer(d, 0)

    z_peer = edge_peer(0, 1)
    c_peer = (sys_id, y * 4 + zl * 2 + (1 - c))

    inputs = []

    def fetch(src, dst):
        cp = pltpu.make_async_copy(src, dst, local_sem.at[len(inputs)])
        cp.start()
        inputs.append(cp)
        return cp

    atoms_in = fetch(atoms_hbm, at_all.at[y, zl, c])
    cot_in = [
        fetch(cot_hbm.at[:, start : start + size], per_chunk[k]["cots"].at[y, zl, c])
        for k, (start, size) in enumerate(chunks)
    ]
    coef_in = fetch(coef_hbm, coef)
    experts_in = fetch(experts_hbm, experts)
    index_in = [
        fetch(src_rows_hbm, src_rows),
        fetch(tgt_rows_hbm, tgt_rows),
        fetch(src_line_hbm, src_line),
        fetch(tgt_line_hbm, tgt_line),
    ]
    radial_in = fetch(radial_hbm, radial)

    barrier = pltpu.get_barrier_semaphore()
    peers = [sys_peer(dz, dx) for dz, dx in SYS_STEPS] + [edge_peer(dy, dz) for dy, dz in EDGE_STEPS] + [c_peer]
    for p in peers:
        pl.semaphore_signal(barrier, inc=1, device_id=p, device_id_type=MESH)
    pl.semaphore_wait(barrier, len(peers))

    sent, groups = [], []

    class Group:
        def __init__(self, copies, landing):
            i = len(groups)
            groups.append(self)
            for src, dst, peer in copies:
                j = len(sent)
                if j >= SEND_SLOTS:
                    sent[j - SEND_SLOTS].wait_send()
                cp = pltpu.make_async_remote_copy(
                    src_ref=src,
                    dst_ref=dst,
                    send_sem=send_sem.at[j % SEND_SLOTS],
                    recv_sem=recv_sem.at[i],
                    device_id=peer,
                    device_id_type=MESH,
                )
                cp.start()
                sent.append(cp)
            self.all = pltpu.make_async_remote_copy(
                src_ref=landing,
                dst_ref=landing,
                send_sem=send_sem.at[0],
                recv_sem=recv_sem.at[i],
                device_id=c_peer,
                device_id_type=MESH,
            )

        def wait_recv(self):
            self.all.wait_recv()

    def send(src, dst, peer):
        return Group([(src, dst, peer)], dst)

    def send_all(block_of, landing, peers):
        return [Group([(block_of(*p), landing.at[i], peer) for i, (p, peer) in enumerate(peers)], landing)]

    y_peers = [((d,), y_peer(d)) for d in SHIFTS]
    x_peers = [((dx,), sys_peer(0, dx)) for dx in SHIFTS]
    edge_peers = [((dy, dz), edge_peer(dy, dz)) for dy, dz in EDGE_STEPS]
    sys_peers = [((dz, dx), sys_peer(dz, dx)) for dz, dx in SYS_STEPS]

    def share(full, cut):
        lo = full.at[:, :, :, 0:cut]
        own = lo.at[y, zl, c]
        m = {"full": full, "lo": lo, "y": []}
        if cut < full.shape[3]:
            m["hi"] = full.at[:, :, :, cut : full.shape[3]]
            block = m["hi"].at[y, zl, c]
            m["yh"] = [Group([(block, block, p) for _, p in y_peers], m["hi"].at[0:3, 0, 0])]
        m["z"] = send(own, own, z_peer)
        m["y"].append(Group([(own, own, p) for _, p in y_peers], lo.at[0:3, 0, 0]))
        return m

    def share_forward(m):
        m["z"].wait_recv()
        other = m["lo"].at[y, 1 - zl, c]
        m["y"].append(Group([(other, other, p) for _, p in y_peers], m["lo"].at[0:3, 0, 0]))

    def share_across(m):
        for cp in m["yh"]:
            cp.wait_recv()
        column = m["hi"].at[:, zl, c]
        m["y"].append(send(column, column, z_peer))

    def share_core(m):
        for cp in m["y"]:
            cp.wait_recv()
        half = m["full"].at[:, :, c]
        m["c"] = send(half, half, c_peer)

    def share_wait(m):
        m["c"].wait_recv()

    e_x, e_z, merged_at, cots_at = ([None] * n for _ in range(4))

    def expert_part(k):
        start, size = chunks[k]
        b = per_chunk[k]
        for i, dx in enumerate(SHIFTS + (0,)):
            for z in range(2):
                to = z * NX + (x + dx) % NX
                total = jnp.zeros((rows, size), F32)
                for e in range(n_exp):
                    total += coef[to, sys_id * n_exp + e] * experts[e, :, start : start + size].astype(F32)
                b["epart"][i, z] = total.astype(BF16)
        if k == 0:
            e_z[0] = send_all(
                lambda dz, dx: b["epart"].at[(SHIFTS + (0,)).index(dx), (zh + dz) % 2], b["ez"], sys_peers
            )
        else:
            e_x[k] = send_all(lambda dx: b["epart"].at[SHIFTS.index(dx)], b["erecv"], x_peers)

    def expert_x(k):
        b = per_chunk[k]
        for cp in e_x[k]:
            cp.wait_recv()
        total = b["epart"][3].astype(F32)
        for i in range(3):
            total += b["erecv"][i].astype(F32)
        b["esum"][...] = total.astype(BF16)
        e_z[k] = [send(b["esum"].at[1 - zh], b["ez"].at[0], sys_peer(1, 0))]

    def merge(k):
        b = per_chunk[k]
        for cp in e_z[k]:
            cp.wait_recv()
        own = b["epart"].at[3] if k == 0 else b["esum"]
        total = own[pl.ds(zh, 1)][0].astype(F32)
        for i in range(b["ez"].shape[0]):
            total += b["ez"][i].astype(F32)
        b["merged"][pl.ds(y, 1), pl.ds(zl, 1), pl.ds(c, 1)] = total.astype(BF16)[None, None, None]
        merged_at[k] = share(b["merged"], 48 if k == 0 else rows)
        if k > 0:
            cots_at[k] = share(b["cots"], own_atoms)

    def merge_forward(k):
        share_forward(merged_at[k])
        share_forward(cots_at[k])

    def merge_core(k):
        share_core(merged_at[k])

    def cots_core(k):
        share_core(cots_at[k])

    def merge_wait(k):
        share_wait(merged_at[k])

    def cots_wait(k):
        share_wait(cots_at[k])

    def one_hots():
        lane = lax.broadcasted_iota(jnp.int32, (128, 128), 1)

        def by_edge(j, _):
            at = pl.ds(pl.multiple_of(j * 128, 128), 128)
            for idx, out in ((src_rows, oh_src), (tgt_rows, oh_tgt)):
                col = jnp.broadcast_to(idx[pl.ds(j, 1), :], (128, 128)).T
                for a in range(n_atoms // 128):
                    out[at, a * 128 : (a + 1) * 128] = jnp.where(col == lane + a * 128, 1.0, 0.0).astype(BF16)
            return 0

        lax.fori_loop(0, n_edges // 128, by_edge, 0)
        sub = lax.broadcasted_iota(jnp.int32, (64, n_edges), 0)

        def by_atom(j, _):
            at = pl.ds(pl.multiple_of(j * 64, 64), 64)
            for idx, out in ((src_line, ot_src), (tgt_line, ot_tgt)):
                line = jnp.broadcast_to(idx[...], (64, n_edges)) - j * 64
                out[at, :] = jnp.where(line == sub, 1.0, 0.0).astype(BF16)
            return 0

        lax.fori_loop(0, n_atoms // 64, by_atom, 0)

    def select_atoms():
        count = 4 * rows
        i = lax.broadcasted_iota(jnp.int32, (count, width), 0)
        j = lax.broadcasted_iota(jnp.int32, (count, width), 1)
        pick = jnp.where(j == i + (i // rows + c) * rows, 1.0, 0.0).astype(BF16)
        sel_atoms[...] = dot_t(pick, at_all[...].reshape(n_atoms, width)).astype(BF16)

    def project(k):
        size = chunks[k][1]
        b = per_chunk[k]
        narrow = 2 * size <= proj.shape[2]

        def body(t, _):
            at = pl.ds(pl.multiple_of(t * 256, 256), 256)
            a = at_all[pl.ds(t, 1)].reshape(256, width)
            w = [b["merged"][2 * h : 2 * h + 2].reshape(width, size) for h in range(2)]
            if narrow:
                both = dot(a, jnp.concatenate(w, axis=1)).astype(BF16)
                proj[0, at, 0:size] = both[:, 0:size]
                proj[1, at, 0:size] = both[:, size : 2 * size]
                proj[1, at, size : 2 * size] = b["cots"][pl.ds(t, 1)].reshape(256, size)
            else:
                for h in range(2):
                    proj[h, at, 0:size] = dot(a, w[h]).astype(BF16)
            return 0

        lax.fori_loop(0, NY, body, 0)

    def pick(k, half):
        start, size = chunks[k]
        b = per_chunk[k]
        narrow = 2 * size <= proj.shape[2]
        count = n_edges // 1024

        def body(t, _):
            at = pl.ds(pl.multiple_of(t * 512, 512), 512)
            o_s, o_t = oh_src[at, :], oh_tgt[at, :]
            if narrow:
                by_tgt = dot(o_t, proj[1, :, 0 : 2 * size])
                edge_cot = by_tgt[:, size : 2 * size]
                pre = dot(o_s, proj[0, :, 0:size]) + by_tgt[:, 0:size]
            else:
                pre = dot(o_s, proj[0, :, 0:size]) + dot(o_t, proj[1, :, 0:size])
                edge_cot = dot(o_t, b["cots"][...].reshape(n_atoms, size))
            r = radial[at, start : start + size].astype(F32)
            g = 1.0 / (1.0 + jnp.exp(-pre))
            edge_vals[at, 0:size] = (edge_cot * r * (g * (1.0 + pre * (1.0 - g)))).astype(BF16)
            edge_vals[at, size : 2 * size] = (pre * g * r).astype(BF16)
            return 0

        lax.fori_loop(half * count, (half + 1) * count, body, 0)

    c_recv = [None] * n

    def sums(k, tiles):
        size = chunks[k][1]
        b = per_chunk[k]
        if c_recv[k] is None:
            c_recv[k] = []
        for d in tiles:
            pair = (y // 2 + d) % 2
            at = pl.ds(pl.multiple_of(pair * (n_atoms // 2), n_atoms // 2), n_atoms // 2)
            o_s, o_t = ot_src[at, :], ot_tgt[at, :]
            by_src = dot(o_s, edge_vals[:, 0:size]).astype(BF16)
            by_tgt = dot(o_t, edge_vals[:, 0 : 2 * size]).astype(BF16)
            spot = pl.ds(pair * 2, 2)
            b["sums"][spot, :, :, :, 0:size] = by_src.reshape(2, 2, 2, own_atoms, size)
            b["sums"][spot, :, :, :, size : 3 * size] = by_tgt.reshape(2, 2, 2, own_atoms, 2 * size)
            c_recv[k].append((pair, send(b["sums"].at[spot], b["csums"].at[spot], c_peer)))

    w_z, w_y, g_z, g_y, n_y, n_z, d_z, d_x = ([None] * n for _ in range(8))

    def atoms_of(dy, dz):
        return (y + dy) % NY, (zl + dz) % 2

    def reduce_core(k):
        size = chunks[k][1]
        b = per_chunk[k]
        for pair, cp in c_recv[k]:
            cp.wait_recv()
            spot = pl.ds(pair * 2, 2)
            both = b["sums"][spot, :, :, :, 0 : 2 * size].astype(F32) + b["csums"][spot, :, :, :, 0 : 2 * size].astype(F32)
            b["chip"][spot] = both.astype(BF16)
        grad = dot(sel_atoms[...], b["chip"][...].reshape(n_atoms, 2 * size)).astype(BF16)
        b["wpart"][0:2] = grad[:, 0:size].reshape(2, 2, rows, size)
        b["wpart"][2:4] = grad[:, size : 2 * size].reshape(2, 2, rows, size)
        if k > 1:
            w_y[k] = send_all(lambda dy, dz: b["wpart"].at[atoms_of(dy, dz)], b["wd"], edge_peers)
        else:
            w_z[k] = send(b["wpart"].at[:, 1 - zl], b["wz"], z_peer)

    def node_core(k):
        size = chunks[k][1]
        b = per_chunk[k]
        spot = (slice(None), slice(None), pl.ds(c, 1), slice(None), slice(2 * size, 3 * size))
        both = b["sums"][spot].astype(F32) + b["csums"][spot].astype(F32)
        b["nchip"][...] = both.astype(BF16).reshape(NY, 2, own_atoms, size)
        n_y[k] = send_all(lambda d: b["nchip"].at[(y + d) % NY], b["ny"], y_peers)

    def node_z(k):
        b = per_chunk[k]
        for cp in n_y[k]:
            cp.wait_recv()
        total = b["nchip"][pl.ds(y, 1)][0].astype(F32)
        for i in range(3):
            total += b["ny"][i].astype(F32)
        b["nsum"][...] = total.astype(BF16)
        n_z[k] = send(b["nsum"].at[1 - zl], b["nz"], z_peer)

    def node_finish(k):
        start, size = chunks[k]
        b = per_chunk[k]
        n_z[k].wait_recv()
        total = b["nsum"][pl.ds(zl, 1)][0].astype(F32) + b["nz"][...].astype(F32)
        node_out[:, start : start + size] = total.astype(BF16)

    def atom_send(k):
        b = per_chunk[k]
        if k in Z_FIRST:
            g_z[k] = send(b["chip"].at[:, 1 - zl, c], b["gz"], z_peer)
        elif k < 3:
            g_y[k] = send_all(lambda d: b["chip"].at[(y + d) % NY, :, c], b["gd"], y_peers)
        else:
            g_y[k] = send_all(lambda dy, dz: b["chip"].at[(*atoms_of(dy, dz), c)], b["gd"], edge_peers)

    def atom_forward(k):
        size = chunks[k][1]
        b = per_chunk[k]
        if k in Z_FIRST:
            g_z[k].wait_recv()
            own = b["chip"][:, pl.ds(zl, 1), pl.ds(c, 1)].reshape(NY, own_atoms, 2 * size)
            b["gsum"][...] = (own.astype(F32) + b["gz"][...].astype(F32)).astype(BF16)
            g_y[k] = send_all(lambda d: b["gsum"].at[(y + d) % NY], b["gd"], y_peers)
        else:
            g_y[k][0].wait_recv()
            total = b["chip"][pl.ds(y, 1), :, pl.ds(c, 1)].reshape(2, own_atoms, 2 * size).astype(F32)
            for i in range(3):
                total += b["gd"][i].astype(F32)
            b["gsum"][...] = total.astype(BF16)
            g_z[k] = send(b["gsum"].at[1 - zl], b["gz"].at[0], z_peer)

    def atom_finish(k):
        size = chunks[k][1]
        b = per_chunk[k]
        if k not in Z_FIRST and k < 3:
            g_z[k].wait_recv()
            total = b["gsum"][pl.ds(zl, 1)][0].astype(F32) + b["gz"][0].astype(F32)
        else:
            g_y[k][0].wait_recv()
            if k in Z_FIRST:
                total = b["gsum"][pl.ds(y, 1)][0].astype(F32)
            else:
                total = b["chip"][pl.ds(y, 1), pl.ds(zl, 1), pl.ds(c, 1)][0, 0, 0].astype(F32)
            for i in range(b["gd"].shape[0]):
                total += b["gd"][i].astype(F32)
        g = total.astype(BF16)
        grad = dot_t(g[:, 0:size], b["merged"][0:2].reshape(width, size))
        grad += dot_t(g[:, size : 2 * size], b["merged"][2:4].reshape(width, size))
        if k == 0:
            atom_grad[...] = grad
        else:
            atom_grad[...] += grad

    def weight_z(k):
        size = chunks[k][1]
        b = per_chunk[k]
        w_z[k].wait_recv()
        own = b["wpart"][:, pl.ds(zl, 1)].reshape(NY, rows, size)
        b["wsum"][...] = (own.astype(F32) + b["wz"][...].astype(F32)).astype(BF16)
        w_y[k] = send_all(lambda d: b["wsum"].at[(y + d) % NY], b["wd"], y_peers)

    def weight_finish(k):
        b = per_chunk[k]
        for cp in w_y[k]:
            cp.wait_recv()
        if k > 1:
            total = b["wpart"][pl.ds(y, 1), pl.ds(zl, 1)][0].astype(F32)
        else:
            total = b["wsum"][pl.ds(y, 1)].astype(F32)
        for i in range(b["wd"].shape[0]):
            total += b["wd"][i : i + 1].astype(F32)
        b["dall"][pl.ds(sys_id, 1)] = total.astype(BF16)
        own = b["dall"].at[sys_id]
        if k == n - 1:
            d_x[k] = [Group([(own, own, p) for _, p in sys_peers], b["dall"].at[0:7])]
        else:
            d_z[k] = send(own, own, sys_peer(1, 0))
            d_x[k] = [Group([(own, own, p) for _, p in x_peers], b["dall"].at[0:3])]

    def expert_forward(k):
        d_z[k].wait_recv()
        other = per_chunk[k]["dall"].at[(1 - zh) * NX + x]
        d_x[k].append(Group([(other, other, p) for _, p in x_peers], per_chunk[k]["dall"].at[0:3]))

    def expert_finish(k):
        start, size = chunks[k]
        b = per_chunk[k]
        for cp in d_x[k]:
            cp.wait_recv()
        for e in range(n_exp):
            total = jnp.zeros((rows, size), F32)
            for s in range(2 * NX):
                total += coef[s, sys_id * n_exp + e] * b["dall"][s].astype(F32)
            expert_grad[e, :, start : start + size] = total
        cols = slice(start, start + size)
        outputs.append(fetch(expert_grad.at[:, :, cols], expert_hbm.at[:, :, cols]))

    outputs = []
    atoms_in.wait()
    atoms_at = share(at_all, own_atoms // 2)
    for cp in cot_in:
        cp.wait()
    cots_at[0] = share(per_chunk[0]["cots"], own_atoms // 2)
    coef_in.wait()
    experts_in.wait()
    for k in range(n):
        expert_part(k)
    for cp in index_in:
        cp.wait()
    one_hots()
    share_forward(atoms_at)
    share_forward(cots_at[0])
    share_across(atoms_at)
    share_across(cots_at[0])
    merge(0)
    share_forward(merged_at[0])
    expert_x(1)
    share_core(atoms_at)
    share_across(merged_at[0])
    share_core(cots_at[0])
    share_wait(atoms_at)
    select_atoms()
    share_core(merged_at[0])
    radial_in.wait()
    merge(1)
    cots_wait(0)
    merge_wait(0)

    work = (
        project,
        lambda k: pick(k, 0),
        lambda k: pick(k, 1),
        lambda k: sums(k, (1,)),
        lambda k: sums(k, (0,)),
    )
    beside = {
        (0, 0): ((expert_x, 2),),
        (0, 1): ((merge_forward, 1),),
        (0, 2): ((expert_x, 3),),
        (0, 3): ((merge, 2),),
        (0, 4): (
            (merge_core, 1),
            (cots_core, 1),
            (merge_forward, 2),
            (merge, 3),
            (reduce_core, 0),
            (node_core, 0),
            (merge_wait, 1),
        ),
        (1, 0): ((cots_wait, 1), (atom_send, 0)),
        (1, 1): ((merge_forward, 3),),
        (1, 2): ((merge_core, 2), (cots_core, 2)),
        (1, 3): ((merge_wait, 2), (cots_wait, 2)),
        (1, 4): ((weight_z, 0),),
        (2, 0): ((reduce_core, 1), (node_core, 1), (atom_send, 1), (atom_forward, 0)),
        (2, 2): ((merge_core, 3), (cots_core, 3), (weight_finish, 0)),
        (2, 3): ((merge_wait, 3), (cots_wait, 3), (node_z, 0), (weight_z, 1)),
        (3, 0): ((reduce_core, 2), (atom_send, 2), (node_core, 2), (expert_forward, 0)),
        (3, 2): ((node_z, 1),),
        (3, 3): ((weight_finish, 1),),
        (3, 4): ((atom_forward, 1), (atom_finish, 0)),
    }
    for k in range(n):
        for slot, f in enumerate(work):
            f(k)
            for g, i in beside.get((k, slot), ()):
                g(i)
    reduce_core(3)
    weight_finish(2)
    node_core(3)
    atom_send(3)
    atom_forward(2)
    expert_finish(0)
    expert_forward(1)
    node_z(2)
    weight_finish(3)
    expert_forward(2)
    atom_finish(1)
    node_z(3)
    expert_finish(1)
    for k in range(n):
        node_finish(k)
    outputs.append(fetch(node_out, node_hbm))
    atom_finish(2)
    atom_finish(3)
    outputs.append(fetch(atom_grad, atom_hbm))
    expert_finish(2)
    expert_finish(3)

    def finish():
        for cp in outputs:
            cp.wait()

    def drain():
        for cp in sent[-SEND_SLOTS:]:
            cp.wait_send()
        assert len(groups) == recv_sem.shape[0], len(groups)

    finish()
    drain()


def write_out(*refs):
    count = (len(refs) - 1) // 3
    sem = refs[-1]
    moves = []
    for src, dst, buf in zip(refs[:count], refs[count : 2 * count], refs[2 * count : 3 * count]):
        for i in range(src.shape[0]):
            moves.append((src.at[i], buf.at[i], dst.at[i]))
    reads = [pltpu.make_async_copy(s, b, sem.at[0, i]) for i, (s, b, _) in enumerate(moves)]
    writes = [pltpu.make_async_copy(b, d, sem.at[1, i]) for i, (_, b, d) in enumerate(moves)]
    for r in reads:
        r.start()
    for r, w in zip(reads, writes):
        r.wait()
        w.start()
    for w in writes:
        w.wait()


def layer(atoms, cotangent, experts, radial, coef, source, target):
    n_exp, rows, width = experts.shape
    own = atoms.shape[1]
    n_atoms = 16 * own
    n_edges = radial.shape[1]
    chunks, at = [], 0
    while at < width:
        size = min(256, width - at)
        chunks.append((at, size))
        at += size

    def vmem(*shape):
        return pltpu.VMEM(shape, BF16)

    per_chunk = [
        {
            "epart": vmem(4, 2, rows, s),
            "erecv": vmem(3, 2, rows, s),
            "esum": vmem(2, rows, s),
            "ez": vmem(7 if k == 0 else 1, rows, s),
            "cots": vmem(NY, 2, 2, own, s),
            "merged": vmem(NY, 2, 2, rows, s),
            "sums": vmem(NY, 2, 2, own, 3 * s),
            "csums": vmem(NY, 2, 2, own, 3 * s),
            "chip": vmem(NY, 2, 2, own, 2 * s),
            "nchip": vmem(NY, 2, own, s),
            "ny": vmem(3, 2, own, s),
            "nsum": vmem(2, own, s),
            "nz": vmem(own, s),
            "gz": vmem(NY if k in Z_FIRST else 1, own, 2 * s),
            "gsum": vmem(NY if k in Z_FIRST else 2, own, 2 * s),
            "gd": vmem(*((3,) if k in Z_FIRST else (3, 2) if k < 3 else (7,)), own, 2 * s),
            "wpart": vmem(NY, 2, rows, s),
            "wz": vmem(NY, rows, s),
            "wsum": vmem(NY, rows, s),
            "wd": vmem(7 if k > 1 else 3, rows, s),
            "dall": vmem(8, rows, s),
        }
        for k, (_, s) in enumerate(chunks)
    ]
    wide = max(s for _, s in chunks)
    hbm = pl.BlockSpec(memory_space=pl.ANY)
    node, agrad, egrad = pl.pallas_call(
        functools.partial(kernel, chunks),
        out_shape=(
            jax.ShapeDtypeStruct((own, width), BF16),
            jax.ShapeDtypeStruct((own, width), F32),
            jax.ShapeDtypeStruct((n_exp, rows, width), F32),
        ),
        in_specs=[hbm] * 9,
        out_specs=(hbm, hbm, hbm),
        scratch_shapes=[
            vmem(own, width),
            pltpu.VMEM((own, width), F32),
            pltpu.VMEM((n_exp, rows, width), F32),
            pltpu.SMEM(coef.shape, F32),
            pltpu.VMEM((n_edges // 128, 128), jnp.int32),
            pltpu.VMEM((n_edges // 128, 128), jnp.int32),
            pltpu.VMEM((1, n_edges), jnp.int32),
            pltpu.VMEM((1, n_edges), jnp.int32),
            vmem(n_exp, rows, width),
            vmem(n_edges, width),
            vmem(NY, 2, 2, own, width),
            vmem(n_edges, n_atoms),
            vmem(n_edges, n_atoms),
            vmem(n_atoms, n_edges),
            vmem(n_atoms, n_edges),
            vmem(4 * rows, n_atoms),
            vmem(2, n_atoms, wide),
            vmem(n_edges, 2 * wide),
            per_chunk,
            pltpu.SemaphoreType.DMA((10 + 2 * len(chunks),)),
            pltpu.SemaphoreType.DMA((SEND_SLOTS,)),
            pltpu.SemaphoreType.DMA((RECV_SLOTS,)),
        ],
        compiler_params=pltpu.CompilerParams(
            collective_id=0, has_side_effects=True, vmem_limit_bytes=67043328
        ),
    )(
        experts,
        coef,
        atoms[0],
        cotangent[0],
        radial[0],
        source.reshape(n_edges // 128, 128),
        target.reshape(n_edges // 128, 128),
        source,
        target,
    )
    results = (node[None], agrad[None], egrad)
    moves = sum(r.shape[0] for r in results)
    return pl.pallas_call(
        write_out,
        out_shape=tuple(jax.ShapeDtypeStruct(r.shape, r.dtype) for r in results),
        in_specs=[hbm] * 3,
        out_specs=(hbm,) * 3,
        scratch_shapes=[pltpu.VMEM(r.shape, r.dtype) for r in results] + [pltpu.SemaphoreType.DMA((2, moves))],
    )(*results)


def solution(mesh):
    spec = P("sys", "edge", None)
    return jax.shard_map(
        layer,
        mesh=mesh,
        in_specs=(spec, spec, spec, spec, P(), P("sys", "edge"), P("sys", "edge")),
        out_specs=(spec, spec, spec),
        check_vma=False,
    )
```

```python
import functools

import jax
import jax.numpy as jnp
from jax import lax
from jax.experimental import pallas as pl
from jax.experimental.pallas import tpu as pltpu
from jax.sharding import PartitionSpec as P

F32 = jnp.float32
BF16 = jnp.bfloat16
MESH = pl.DeviceIdType.MESH
NX, NY = 4, 4
SHIFTS = (2, 1, 3)
SEND_SLOTS = 40
RECV_SLOTS = 89
SYS_STEPS = tuple((dz, dx) for dx in (2, 1, 3, 0) for dz in (1, 0) if (dz, dx) != (0, 0))
EDGE_STEPS = tuple((dy, dz) for dy in (2, 1, 3, 0) for dz in (1, 0) if (dy, dz) != (0, 0))


def dot(a, b):
    return lax.dot_general(a, b, (((1,), (0,)), ((), ())), preferred_element_type=F32)


def dot_t(a, b):
    return lax.dot_general(a, b, (((1,), (1,)), ((), ())), preferred_element_type=F32)


def kernel(
    chunks,
    experts_hbm,
    coef_hbm,
    atoms_hbm,
    cot_hbm,
    radial_hbm,
    src_rows_hbm,
    tgt_rows_hbm,
    src_line_hbm,
    tgt_line_hbm,
    node_hbm,
    atom_hbm,
    expert_hbm,
    node_out,
    atom_grad,
    expert_grad,
    coef,
    src_rows,
    tgt_rows,
    src_line,
    tgt_line,
    experts,
    radial,
    at_all,
    oh_src,
    oh_tgt,
    ot_src,
    ot_tgt,
    sel_atoms,
    proj,
    edge_vals,
    edge_cots,
    per_chunk,
    local_sem,
    send_sem,
    recv_sem,
):
    n_exp, rows, width = experts.shape
    own_atoms = atoms_hbm.shape[0]
    n_atoms = 16 * own_atoms
    n_edges = radial.shape[0]
    n = len(chunks)
    sys_id = lax.axis_index("sys")
    edge_id = lax.axis_index("edge")
    zh, x = sys_id // NX, sys_id % NX
    y, zl, c = edge_id // 4, (edge_id // 2) % 2, edge_id % 2

    def sys_peer(dz, dx):
        return (((zh + dz) % 2) * NX + (x + dx) % NX, edge_id)

    def edge_peer(dy, dz):
        return (sys_id, ((y + dy) % NY) * 4 + ((zl + dz) % 2) * 2 + c)

    def y_peer(d):
        return edge_peer(d, 0)

    z_peer = edge_peer(0, 1)
    c_peer = (sys_id, y * 4 + zl * 2 + (1 - c))

    inputs = []

    def fetch(src, dst):
        cp = pltpu.make_async_copy(src, dst, local_sem.at[len(inputs)])
        cp.start()
        inputs.append(cp)
        return cp

    atoms_in = fetch(atoms_hbm, at_all.at[y, zl, c])
    cot_in = [
        fetch(cot_hbm.at[:, start : start + size], per_chunk[k]["cots"].at[y, zl, c])
        for k, (start, size) in enumerate(chunks)
    ]
    coef_in = fetch(coef_hbm, coef)
    experts_in = fetch(experts_hbm, experts)
    index_in = [
        fetch(src_rows_hbm, src_rows),
        fetch(tgt_rows_hbm, tgt_rows),
        fetch(src_line_hbm, src_line),
        fetch(tgt_line_hbm, tgt_line),
    ]
    radial_in = fetch(radial_hbm, radial)

    barrier = pltpu.get_barrier_semaphore()
    peers = [sys_peer(dz, dx) for dz, dx in SYS_STEPS] + [edge_peer(dy, dz) for dy, dz in EDGE_STEPS] + [c_peer]
    for p in peers:
        pl.semaphore_signal(barrier, inc=1, device_id=p, device_id_type=MESH)
    pl.semaphore_wait(barrier, len(peers))

    sent, groups = [], []

    class Group:
        def __init__(self, copies, landing):
            i = len(groups)
            groups.append(self)
            for src, dst, peer in copies:
                j = len(sent)
                if j >= SEND_SLOTS:
                    sent[j - SEND_SLOTS].wait_send()
                cp = pltpu.make_async_remote_copy(
                    src_ref=src,
                    dst_ref=dst,
                    send_sem=send_sem.at[j % SEND_SLOTS],
                    recv_sem=recv_sem.at[i],
                    device_id=peer,
                    device_id_type=MESH,
                )
                cp.start()
                sent.append(cp)
            self.all = pltpu.make_async_remote_copy(
                src_ref=landing,
                dst_ref=landing,
                send_sem=send_sem.at[0],
                recv_sem=recv_sem.at[i],
                device_id=c_peer,
                device_id_type=MESH,
            )

        def wait_recv(self):
            self.all.wait_recv()

    def send(src, dst, peer):
        return Group([(src, dst, peer)], dst)

    def send_all(block_of, landing, peers):
        return [Group([(block_of(*p), landing.at[i], peer) for i, (p, peer) in enumerate(peers)], landing)]

    y_peers = [((d,), y_peer(d)) for d in SHIFTS]
    x_peers = [((dx,), sys_peer(0, dx)) for dx in SHIFTS]
    edge_peers = [((dy, dz), edge_peer(dy, dz)) for dy, dz in EDGE_STEPS]
    sys_peers = [((dz, dx), sys_peer(dz, dx)) for dz, dx in SYS_STEPS]

    def share(full, cut):
        lo = full.at[:, :, :, 0:cut]
        own = lo.at[y, zl, c]
        m = {"full": full, "lo": lo, "y": []}
        if cut < full.shape[3]:
            m["hi"] = full.at[:, :, :, cut : full.shape[3]]
            block = m["hi"].at[y, zl, c]
            m["yh"] = [Group([(block, block, p) for _, p in y_peers], m["hi"].at[0:3, 0, 0])]
        m["z"] = send(own, own, z_peer)
        m["y"].append(Group([(own, own, p) for _, p in y_peers], lo.at[0:3, 0, 0]))
        return m

    def share_forward(m):
        m["z"].wait_recv()
        other = m["lo"].at[y, 1 - zl, c]
        m["y"].append(Group([(other, other, p) for _, p in y_peers], m["lo"].at[0:3, 0, 0]))

    def share_across(m):
        for cp in m["yh"]:
            cp.wait_recv()
        column = m["hi"].at[:, zl, c]
        m["y"].append(send(column, column, z_peer))

    def share_core(m):
        for cp in m["y"]:
            cp.wait_recv()
        half = m["full"].at[:, :, c]
        m["c"] = send(half, half, c_peer)

    def share_wait(m):
        m["c"].wait_recv()

    e_x, e_z, merged_at, cots_at = ([None] * n for _ in range(4))

    def expert_part(k):
        start, size = chunks[k]
        b = per_chunk[k]
        for i, dx in enumerate(SHIFTS + (0,)):
            for z in range(2):
                to = z * NX + (x + dx) % NX
                total = jnp.zeros((rows, size), F32)
                for e in range(n_exp):
                    total += coef[to, sys_id * n_exp + e] * experts[e, :, start : start + size].astype(F32)
                b["epart"][i, z] = total.astype(BF16)
        if k == 0:
            e_z[0] = send_all(
                lambda dz, dx: b["epart"].at[(SHIFTS + (0,)).index(dx), (zh + dz) % 2], b["ez"], sys_peers
            )
        else:
            e_x[k] = send_all(lambda dx: b["epart"].at[SHIFTS.index(dx)], b["erecv"], x_peers)

    def expert_x(k):
        b = per_chunk[k]
        for cp in e_x[k]:
            cp.wait_recv()
        total = b["epart"][3].astype(F32)
        for i in range(3):
            total += b["erecv"][i].astype(F32)
        b["esum"][...] = total.astype(BF16)
        e_z[k] = [send(b["esum"].at[1 - zh], b["ez"].at[0], sys_peer(1, 0))]

    def merge(k):
        b = per_chunk[k]
        for cp in e_z[k]:
            cp.wait_recv()
        own = b["epart"].at[3] if k == 0 else b["esum"]
        total = own[pl.ds(zh, 1)][0].astype(F32)
        for i in range(b["ez"].shape[0]):
            total += b["ez"][i].astype(F32)
        b["merged"][pl.ds(y, 1), pl.ds(zl, 1), pl.ds(c, 1)] = total.astype(BF16)[None, None, None]
        merged_at[k] = share(b["merged"], rows * 3 // 7 if k == 0 else rows)
        if k > 1:
            cots_at[k] = share(b["cots"], own_atoms)

    def merge_forward(k):
        if k == 1:
            share_forward(cots_at[k])
        share_forward(merged_at[k])
        if k > 1:
            share_forward(cots_at[k])

    def merge_core(k):
        share_core(merged_at[k])

    def cots_core(k):
        share_core(cots_at[k])

    def merge_wait(k):
        share_wait(merged_at[k])

    def cots_wait(k):
        share_wait(cots_at[k])

    def one_hots():
        lane = lax.broadcasted_iota(jnp.int32, (128, 128), 1)

        def by_edge(j, _):
            at = pl.ds(pl.multiple_of(j * 128, 128), 128)
            for idx, out in ((src_rows, oh_src), (tgt_rows, oh_tgt)):
                col = jnp.broadcast_to(idx[pl.ds(j, 1), :], (128, 128)).T
                for a in range(n_atoms // 128):
                    out[at, a * 128 : (a + 1) * 128] = jnp.where(col == lane + a * 128, 1.0, 0.0).astype(BF16)
            return 0

        lax.fori_loop(0, n_edges // 128, by_edge, 0)
        sub = lax.broadcasted_iota(jnp.int32, (64, n_edges), 0)

        def by_atom(j, _):
            at = pl.ds(pl.multiple_of(j * 64, 64), 64)
            for idx, out in ((src_line, ot_src), (tgt_line, ot_tgt)):
                line = jnp.broadcast_to(idx[...], (64, n_edges)) - j * 64
                out[at, :] = jnp.where(line == sub, 1.0, 0.0).astype(BF16)
            return 0

        lax.fori_loop(0, n_atoms // 64, by_atom, 0)

    def select_atoms():
        count = 4 * rows
        i = lax.broadcasted_iota(jnp.int32, (count, width), 0)
        j = lax.broadcasted_iota(jnp.int32, (count, width), 1)
        pick = jnp.where(j == i + (i // rows + c) * rows, 1.0, 0.0).astype(BF16)
        sel_atoms[...] = dot_t(pick, at_all[...].reshape(n_atoms, width)).astype(BF16)

    def project(k):
        size = chunks[k][1]
        b = per_chunk[k]
        narrow = 2 * size <= proj.shape[2]

        def body(t, _):
            at = pl.ds(pl.multiple_of(t * 256, 256), 256)
            a = at_all[pl.ds(t, 1)].reshape(256, width)
            w = [b["merged"][2 * h : 2 * h + 2].reshape(width, size) for h in range(2)]
            if narrow:
                both = dot(a, jnp.concatenate(w, axis=1)).astype(BF16)
                proj[0, at, 0:size] = both[:, 0:size]
                proj[1, at, 0:size] = both[:, size : 2 * size]
                proj[1, at, size : 2 * size] = b["cots"][pl.ds(t, 1)].reshape(256, size)
            else:
                for h in range(2):
                    proj[h, at, 0:size] = dot(a, w[h]).astype(BF16)
            return 0

        lax.fori_loop(0, NY, body, 0)

    def pick_first():
        size = chunks[0][1]
        b = per_chunk[0]

        def body(t, _):
            at = pl.ds(pl.multiple_of(t * 512, 512), 512)
            edge_cots[at, :] = dot(oh_tgt[at, :], b["cots"][...].reshape(n_atoms, size)).astype(BF16)
            return 0

        lax.fori_loop(0, n_edges // 512, body, 0)

    def pick(k, half):
        start, size = chunks[k]
        b = per_chunk[k]
        narrow = 2 * size <= proj.shape[2]
        count = n_edges // 1024

        def body(t, _):
            at = pl.ds(pl.multiple_of(t * 512, 512), 512)
            o_s, o_t = oh_src[at, :], oh_tgt[at, :]
            if narrow:
                by_tgt = dot(o_t, proj[1, :, 0 : 2 * size])
                edge_cot = by_tgt[:, size : 2 * size]
                pre = dot(o_s, proj[0, :, 0:size]) + by_tgt[:, 0:size]
            else:
                pre = dot(o_s, proj[0, :, 0:size]) + dot(o_t, proj[1, :, 0:size])
                if k == 0:
                    edge_cot = edge_cots[at, :].astype(F32)
                else:
                    edge_cot = dot(o_t, b["cots"][...].reshape(n_atoms, size))
            r = radial[at, start : start + size].astype(F32)
            g = 1.0 / (1.0 + jnp.exp(-pre))
            edge_vals[at, 0:size] = (edge_cot * r * (g * (1.0 + pre * (1.0 - g)))).astype(BF16)
            edge_vals[at, size : 2 * size] = (pre * g * r).astype(BF16)
            return 0

        lax.fori_loop(half * count, (half + 1) * count, body, 0)

    c_recv = [None] * n

    def sums(k, tiles):
        size = chunks[k][1]
        b = per_chunk[k]
        if c_recv[k] is None:
            c_recv[k] = []
        for d in tiles:
            pair = (y // 2 + d) % 2
            at = pl.ds(pl.multiple_of(pair * (n_atoms // 2), n_atoms // 2), n_atoms // 2)
            o_s, o_t = ot_src[at, :], ot_tgt[at, :]
            by_src = dot(o_s, edge_vals[:, 0:size]).astype(BF16)
            by_tgt = dot(o_t, edge_vals[:, 0 : 2 * size]).astype(BF16)
            spot = pl.ds(pair * 2, 2)
            b["sums"][spot, :, :, :, 0:size] = by_src.reshape(2, 2, 2, own_atoms, size)
            b["sums"][spot, :, :, :, size : 3 * size] = by_tgt.reshape(2, 2, 2, own_atoms, 2 * size)
            c_recv[k].append((pair, send(b["sums"].at[spot], b["csums"].at[spot], c_peer)))

    w_z, w_y, g_z, g_y, n_y, n_z, d_z, d_x = ([None] * n for _ in range(8))

    h_y = []

    def atoms_of(dy, dz):
        return (y + dy) % NY, (zl + dz) % 2

    def reduce_core(k):
        size = chunks[k][1]
        b = per_chunk[k]
        for pair, cp in c_recv[k]:
            cp.wait_recv()
            spot = pl.ds(pair * 2, 2)
            both = b["sums"][spot, :, :, :, 0 : 2 * size].astype(F32) + b["csums"][spot, :, :, :, 0 : 2 * size].astype(F32)
            b["chip"][spot] = both.astype(BF16)
        grad = dot(sel_atoms[...], b["chip"][...].reshape(n_atoms, 2 * size)).astype(BF16)
        b["wpart"][0:2] = grad[:, 0:size].reshape(2, 2, rows, size)
        b["wpart"][2:4] = grad[:, size : 2 * size].reshape(2, 2, rows, size)
        if k > 0:
            w_y[k] = send_all(lambda dy, dz: b["wpart"].at[atoms_of(dy, dz)], b["wd"], edge_peers)
        else:
            w_z[k] = send(b["wpart"].at[:, 1 - zl], b["wz"], z_peer)

    def node_core(k):
        size = chunks[k][1]
        b = per_chunk[k]
        spot = (slice(None), slice(None), pl.ds(c, 1), slice(None), slice(2 * size, 3 * size))
        both = b["sums"][spot].astype(F32) + b["csums"][spot].astype(F32)
        b["nchip"][...] = both.astype(BF16).reshape(NY, 2, own_atoms, size)
        n_y[k] = send_all(lambda d: b["nchip"].at[(y + d) % NY], b["ny"], y_peers)

    def node_z(k):
        b = per_chunk[k]
        for cp in n_y[k]:
            cp.wait_recv()
        total = b["nchip"][pl.ds(y, 1)][0].astype(F32)
        for i in range(3):
            total += b["ny"][i].astype(F32)
        b["nsum"][...] = total.astype(BF16)
        n_z[k] = send(b["nsum"].at[1 - zl], b["nz"], z_peer)

    def node_finish(k):
        start, size = chunks[k]
        b = per_chunk[k]
        n_z[k].wait_recv()
        total = b["nsum"][pl.ds(zl, 1)][0].astype(F32) + b["nz"][...].astype(F32)
        node_out[:, start : start + size] = total.astype(BF16)

    def zy_part(k):
        return chunks[k][1] * (1 if k == 2 else 2)

    def atom_send(k):
        b = per_chunk[k]
        part = zy_part(k)
        if k == 3:
            g_y[k] = send_all(lambda dy, dz: b["chip"].at[(*atoms_of(dy, dz), c)], b["gd"], edge_peers)
            return
        g_z[k] = send(b["chip"].at[:, 1 - zl, c, :, 0:part], b["gz"], z_peer)
        if k == 2:
            h_y.extend(send_all(lambda d: b["chip"].at[(y + d) % NY, :, c, :, part : 2 * part], b["hd"], y_peers))

    def atom_forward(k):
        part = zy_part(k)
        b = per_chunk[k]
        g_z[k].wait_recv()
        own = b["chip"][:, pl.ds(zl, 1), pl.ds(c, 1), :, 0:part].reshape(NY, own_atoms, part)
        b["gsum"][...] = (own.astype(F32) + b["gz"][...].astype(F32)).astype(BF16)
        g_y[k] = send_all(lambda d: b["gsum"].at[(y + d) % NY], b["gd"], y_peers)

    def atom_across(k):
        part = zy_part(k)
        b = per_chunk[k]
        h_y[0].wait_recv()
        total = b["chip"][pl.ds(y, 1), :, pl.ds(c, 1), :, part : 2 * part].reshape(2, own_atoms, part).astype(F32)
        for i in range(3):
            total += b["hd"][i].astype(F32)
        b["hsum"][...] = total.astype(BF16)
        h_y.append(send(b["hsum"].at[1 - zl], b["hz"], z_peer))

    def atom_finish(k):
        size = chunks[k][1]
        b = per_chunk[k]
        g_y[k][0].wait_recv()
        if k < 3:
            total = b["gsum"][pl.ds(y, 1)][0].astype(F32)
        else:
            total = b["chip"][pl.ds(y, 1), pl.ds(zl, 1), pl.ds(c, 1)][0, 0, 0].astype(F32)
        for i in range(b["gd"].shape[0]):
            total += b["gd"][i].astype(F32)
        if k == 2:
            h_y[1].wait_recv()
            rest = b["hsum"][pl.ds(zl, 1)][0].astype(F32) + b["hz"][...].astype(F32)
            total = jnp.concatenate([total, rest], axis=1)
        g = total.astype(BF16)
        grad = dot_t(g[:, 0:size], b["merged"][0:2].reshape(width, size))
        grad += dot_t(g[:, size : 2 * size], b["merged"][2:4].reshape(width, size))
        if k == 0:
            atom_grad[...] = grad
        else:
            atom_grad[...] += grad

    def weight_z(k):
        size = chunks[k][1]
        b = per_chunk[k]
        w_z[k].wait_recv()
        own = b["wpart"][:, pl.ds(zl, 1)].reshape(NY, rows, size)
        b["wsum"][...] = (own.astype(F32) + b["wz"][...].astype(F32)).astype(BF16)
        w_y[k] = send_all(lambda d: b["wsum"].at[(y + d) % NY], b["wd"], y_peers)

    def weight_finish(k):
        b = per_chunk[k]
        for cp in w_y[k]:
            cp.wait_recv()
        if k > 0:
            total = b["wpart"][pl.ds(y, 1), pl.ds(zl, 1)][0].astype(F32)
        else:
            total = b["wsum"][pl.ds(y, 1)].astype(F32)
        for i in range(b["wd"].shape[0]):
            total += b["wd"][i : i + 1].astype(F32)
        b["dall"][pl.ds(sys_id, 1)] = total.astype(BF16)
        own = b["dall"].at[sys_id]
        if k == n - 1:
            d_x[k] = [Group([(own, own, p) for _, p in sys_peers], b["dall"].at[0:7])]
        else:
            d_z[k] = send(own, own, sys_peer(1, 0))
            d_x[k] = [Group([(own, own, p) for _, p in x_peers], b["dall"].at[0:3])]

    def expert_forward(k):
        d_z[k].wait_recv()
        other = per_chunk[k]["dall"].at[(1 - zh) * NX + x]
        d_x[k].append(Group([(other, other, p) for _, p in x_peers], per_chunk[k]["dall"].at[0:3]))

    def expert_finish(k):
        start, size = chunks[k]
        b = per_chunk[k]
        for cp in d_x[k]:
            cp.wait_recv()
        for e in range(n_exp):
            total = jnp.zeros((rows, size), F32)
            for s in range(2 * NX):
                total += coef[s, sys_id * n_exp + e] * b["dall"][s].astype(F32)
            expert_grad[e, :, start : start + size] = total
        cols = slice(start, start + size)
        outputs.append(fetch(expert_grad.at[:, :, cols], expert_hbm.at[:, :, cols]))

    outputs = []
    atoms_in.wait()
    atoms_at = share(at_all, own_atoms // 2)
    for cp in cot_in:
        cp.wait()
    cots_at[0] = share(per_chunk[0]["cots"], own_atoms // 2)
    coef_in.wait()
    experts_in.wait()
    for k in range(n):
        expert_part(k)
    for cp in index_in:
        cp.wait()
    one_hots()
    share_forward(atoms_at)
    share_forward(cots_at[0])
    share_across(atoms_at)
    share_across(cots_at[0])
    merge(0)
    share_forward(merged_at[0])
    expert_x(1)
    share_core(atoms_at)
    share_across(merged_at[0])
    share_core(cots_at[0])
    share_wait(atoms_at)
    select_atoms()
    cots_at[1] = share(per_chunk[1]["cots"], own_atoms)
    cots_wait(0)
    pick_first()
    share_core(merged_at[0])
    radial_in.wait()
    merge(1)
    merge_wait(0)

    work = (
        project,
        lambda k: pick(k, 0),
        lambda k: pick(k, 1),
        lambda k: sums(k, (1,)),
        lambda k: sums(k, (0,)),
    )
    beside = {
        (0, 0): ((merge_forward, 1), (expert_x, 2)),
        (0, 2): ((expert_x, 3),),
        (0, 3): ((merge, 2), (merge_core, 1)),
        (0, 4): ((cots_core, 1), (merge_wait, 1)),
        (1, 0): ((merge_forward, 2), (merge, 3), (reduce_core, 0), (node_core, 0), (atom_send, 0), (cots_wait, 1)),
        (1, 1): ((merge_forward, 3),),
        (1, 2): ((merge_core, 2),),
        (1, 3): ((merge_wait, 2), (cots_core, 2)),
        (1, 4): ((weight_z, 0),),
        (2, 0): ((cots_wait, 2), (reduce_core, 1), (node_core, 1), (atom_send, 1)),
        (2, 1): ((atom_forward, 0),),
        (2, 2): ((merge_core, 3), (cots_core, 3), (weight_finish, 0)),
        (2, 3): ((merge_wait, 3), (cots_wait, 3), (node_z, 0)),
        (3, 0): ((weight_finish, 1), (reduce_core, 2), (atom_send, 2)),
        (3, 3): ((expert_forward, 0), (node_z, 1)),
    }
    for k in range(n):
        for slot, f in enumerate(work):
            f(k)
            for g, i in beside.get((k, slot), ()):
                g(i)
    reduce_core(3)
    atom_forward(1)
    expert_forward(1)
    weight_finish(2)
    node_core(2)
    node_core(3)
    atom_send(3)
    atom_across(2)
    atom_finish(0)
    expert_finish(0)
    atom_forward(2)
    weight_finish(3)
    expert_forward(2)
    atom_finish(1)
    node_z(2)
    expert_finish(1)
    node_z(3)
    atom_finish(2)
    for k in range(n):
        node_finish(k)
    outputs.append(fetch(node_out, node_hbm))
    atom_finish(3)
    outputs.append(fetch(atom_grad, atom_hbm))
    expert_finish(2)
    expert_finish(3)

    def finish():
        for cp in outputs:
            cp.wait()

    def drain():
        for cp in sent[-SEND_SLOTS:]:
            cp.wait_send()
        assert len(groups) == recv_sem.shape[0], len(groups)

    finish()
    drain()


def write_out(*refs):
    count = (len(refs) - 1) // 3
    sem = refs[-1]
    moves = []
    for src, dst, buf in zip(refs[:count], refs[count : 2 * count], refs[2 * count : 3 * count]):
        for i in range(src.shape[0]):
            moves.append((src.at[i], buf.at[i], dst.at[i]))
    reads = [pltpu.make_async_copy(s, b, sem.at[0, i]) for i, (s, b, _) in enumerate(moves)]
    writes = [pltpu.make_async_copy(b, d, sem.at[1, i]) for i, (_, b, d) in enumerate(moves)]
    for r in reads:
        r.start()
    for r, w in zip(reads, writes):
        r.wait()
        w.start()
    for w in writes:
        w.wait()


def layer(atoms, cotangent, experts, radial, coef, source, target):
    n_exp, rows, width = experts.shape
    own = atoms.shape[1]
    n_atoms = 16 * own
    n_edges = radial.shape[1]
    chunks, at = [], 0
    while at < width:
        size = min(256, width - at)
        chunks.append((at, size))
        at += size

    def vmem(*shape):
        return pltpu.VMEM(shape, BF16)

    per_chunk = [
        {
            "epart": vmem(4, 2, rows, s),
            "erecv": vmem(3, 2, rows, s),
            "esum": vmem(2, rows, s),
            "ez": vmem(7 if k == 0 else 1, rows, s),
            "cots": vmem(NY, 2, 2, own, s),
            "merged": vmem(NY, 2, 2, rows, s),
            "sums": vmem(NY, 2, 2, own, 3 * s),
            "csums": vmem(NY, 2, 2, own, 3 * s),
            "chip": vmem(NY, 2, 2, own, 2 * s),
            "nchip": vmem(NY, 2, own, s),
            "ny": vmem(3, 2, own, s),
            "nsum": vmem(2, own, s),
            "nz": vmem(own, s),
            "gz": vmem(NY, own, s if k == 2 else 2 * s),
            "gsum": vmem(NY, own, s if k == 2 else 2 * s),
            "gd": vmem(3 if k < 3 else 7, own, s if k == 2 else 2 * s),
            "hd": vmem(3, 2, own, s),
            "hsum": vmem(2, own, s),
            "hz": vmem(own, s),
            "wpart": vmem(NY, 2, rows, s),
            "wz": vmem(NY, rows, s),
            "wsum": vmem(NY, rows, s),
            "wd": vmem(7 if k > 0 else 3, rows, s),
            "dall": vmem(8, rows, s),
        }
        for k, (_, s) in enumerate(chunks)
    ]
    wide = max(s for _, s in chunks)
    hbm = pl.BlockSpec(memory_space=pl.ANY)
    node, agrad, egrad = pl.pallas_call(
        functools.partial(kernel, chunks),
        out_shape=(
            jax.ShapeDtypeStruct((own, width), BF16),
            jax.ShapeDtypeStruct((own, width), F32),
            jax.ShapeDtypeStruct((n_exp, rows, width), F32),
        ),
        in_specs=[hbm] * 9,
        out_specs=(hbm, hbm, hbm),
        scratch_shapes=[
            vmem(own, width),
            pltpu.VMEM((own, width), F32),
            pltpu.VMEM((n_exp, rows, width), F32),
            pltpu.SMEM(coef.shape, F32),
            pltpu.VMEM((n_edges // 128, 128), jnp.int32),
            pltpu.VMEM((n_edges // 128, 128), jnp.int32),
            pltpu.VMEM((1, n_edges), jnp.int32),
            pltpu.VMEM((1, n_edges), jnp.int32),
            vmem(n_exp, rows, width),
            vmem(n_edges, width),
            vmem(NY, 2, 2, own, width),
            vmem(n_edges, n_atoms),
            vmem(n_edges, n_atoms),
            vmem(n_atoms, n_edges),
            vmem(n_atoms, n_edges),
            vmem(4 * rows, n_atoms),
            vmem(2, n_atoms, wide),
            vmem(n_edges, 2 * wide),
            vmem(n_edges, chunks[0][1]),
            per_chunk,
            pltpu.SemaphoreType.DMA((10 + 2 * len(chunks),)),
            pltpu.SemaphoreType.DMA((SEND_SLOTS,)),
            pltpu.SemaphoreType.DMA((RECV_SLOTS,)),
        ],
        compiler_params=pltpu.CompilerParams(
            collective_id=0, has_side_effects=True, vmem_limit_bytes=67043328
        ),
    )(
        experts,
        coef,
        atoms[0],
        cotangent[0],
        radial[0],
        source.reshape(n_edges // 128, 128),
        target.reshape(n_edges // 128, 128),
        source,
        target,
    )
    results = (node[None], agrad[None], egrad)
    moves = sum(r.shape[0] for r in results)
    return pl.pallas_call(
        write_out,
        out_shape=tuple(jax.ShapeDtypeStruct(r.shape, r.dtype) for r in results),
        in_specs=[hbm] * 3,
        out_specs=(hbm,) * 3,
        scratch_shapes=[pltpu.VMEM(r.shape, r.dtype) for r in results] + [pltpu.SemaphoreType.DMA((2, moves))],
    )(*results)


def solution(mesh):
    spec = P("sys", "edge", None)
    return jax.shard_map(
        layer,
        mesh=mesh,
        in_specs=(spec, spec, spec, spec, P(), P("sys", "edge"), P("sys", "edge")),
        out_specs=(spec, spec, spec),
        check_vma=False,
    )
```

```python
import functools

import jax
import jax.numpy as jnp
from jax import lax
from jax.experimental import pallas as pl
from jax.experimental.pallas import tpu as pltpu
from jax.sharding import PartitionSpec as P

F32 = jnp.float32
BF16 = jnp.bfloat16
MESH = pl.DeviceIdType.MESH
NX, NY = 4, 4
SHIFTS = (2, 1, 3)
SEND_SLOTS = 40
RECV_SLOTS = 91
SYS_STEPS = tuple((dz, dx) for dx in (2, 1, 3, 0) for dz in (1, 0) if (dz, dx) != (0, 0))
EDGE_STEPS = tuple((dy, dz) for dy in (2, 1, 3, 0) for dz in (1, 0) if (dy, dz) != (0, 0))


def dot(a, b):
    return lax.dot_general(a, b, (((1,), (0,)), ((), ())), preferred_element_type=F32)


def dot_t(a, b):
    return lax.dot_general(a, b, (((1,), (1,)), ((), ())), preferred_element_type=F32)


def kernel(
    chunks,
    experts_hbm,
    coef_hbm,
    atoms_hbm,
    cot_hbm,
    radial_hbm,
    src_rows_hbm,
    tgt_rows_hbm,
    src_line_hbm,
    tgt_line_hbm,
    node_hbm,
    atom_hbm,
    expert_hbm,
    node_out,
    atom_grad,
    expert_grad,
    coef,
    src_rows,
    tgt_rows,
    src_line,
    tgt_line,
    experts,
    radial,
    at_all,
    oh_src,
    oh_tgt,
    ot_src,
    ot_tgt,
    sel_atoms,
    edge_vals,
    per_chunk,
    local_sem,
    send_sem,
    recv_sem,
):
    n_exp, rows, width = experts.shape
    own_atoms = atoms_hbm.shape[0]
    n_atoms = 16 * own_atoms
    n_edges = radial.shape[0]
    n = len(chunks)
    sys_id = lax.axis_index("sys")
    edge_id = lax.axis_index("edge")
    zh, x = sys_id // NX, sys_id % NX
    y, zl, c = edge_id // 4, (edge_id // 2) % 2, edge_id % 2

    def sys_peer(dz, dx):
        return (((zh + dz) % 2) * NX + (x + dx) % NX, edge_id)

    def edge_peer(dy, dz):
        return (sys_id, ((y + dy) % NY) * 4 + ((zl + dz) % 2) * 2 + c)

    def y_peer(d):
        return edge_peer(d, 0)

    z_peer = edge_peer(0, 1)
    c_peer = (sys_id, y * 4 + zl * 2 + (1 - c))

    edge_cots = per_chunk[n - 2]["proj"]
    inputs = []

    def fetch(src, dst):
        cp = pltpu.make_async_copy(src, dst, local_sem.at[len(inputs)])
        cp.start()
        inputs.append(cp)
        return cp

    atoms_in = fetch(atoms_hbm, at_all.at[y, zl, c])
    cot_in = [
        fetch(cot_hbm.at[:, start : start + size], per_chunk[k]["cots"].at[y, zl, c])
        for k, (start, size) in enumerate(chunks)
    ]
    coef_in = fetch(coef_hbm, coef)
    experts_in = fetch(experts_hbm, experts)
    index_in = [
        fetch(src_rows_hbm, src_rows),
        fetch(tgt_rows_hbm, tgt_rows),
        fetch(src_line_hbm, src_line),
        fetch(tgt_line_hbm, tgt_line),
    ]
    radial_in = fetch(radial_hbm, radial)

    barrier = pltpu.get_barrier_semaphore()
    peers = [sys_peer(dz, dx) for dz, dx in SYS_STEPS] + [edge_peer(dy, dz) for dy, dz in EDGE_STEPS] + [c_peer]
    for p in peers:
        pl.semaphore_signal(barrier, inc=1, device_id=p, device_id_type=MESH)
    pl.semaphore_wait(barrier, len(peers))

    sent, groups = [], []

    class Group:
        def __init__(self, copies, landing):
            i = len(groups)
            groups.append(self)
            for src, dst, peer in copies:
                j = len(sent)
                if j >= SEND_SLOTS:
                    sent[j - SEND_SLOTS].wait_send()
                cp = pltpu.make_async_remote_copy(
                    src_ref=src,
                    dst_ref=dst,
                    send_sem=send_sem.at[j % SEND_SLOTS],
                    recv_sem=recv_sem.at[i],
                    device_id=peer,
                    device_id_type=MESH,
                )
                cp.start()
                sent.append(cp)
            self.all = pltpu.make_async_remote_copy(
                src_ref=landing,
                dst_ref=landing,
                send_sem=send_sem.at[0],
                recv_sem=recv_sem.at[i],
                device_id=c_peer,
                device_id_type=MESH,
            )

        def wait_recv(self):
            self.all.wait_recv()

    def send(src, dst, peer):
        return Group([(src, dst, peer)], dst)

    def send_all(block_of, landing, peers):
        return [Group([(block_of(*p), landing.at[i], peer) for i, (p, peer) in enumerate(peers)], landing)]

    y_peers = [((d,), y_peer(d)) for d in SHIFTS]
    x_peers = [((dx,), sys_peer(0, dx)) for dx in SHIFTS]
    edge_peers = [((dy, dz), edge_peer(dy, dz)) for dy, dz in EDGE_STEPS]
    sys_peers = [((dz, dx), sys_peer(dz, dx)) for dz, dx in SYS_STEPS]

    def share(full, cut):
        lo = full.at[:, :, :, 0:cut]
        own = lo.at[y, zl, c]
        m = {"full": full, "lo": lo, "y": []}
        if cut < full.shape[3]:
            m["hi"] = full.at[:, :, :, cut : full.shape[3]]
            block = m["hi"].at[y, zl, c]
            m["yh"] = [Group([(block, block, p) for _, p in y_peers], m["hi"].at[0:3, 0, 0])]
        m["z"] = send(own, own, z_peer)
        m["y"].append(Group([(own, own, p) for _, p in y_peers], lo.at[0:3, 0, 0]))
        return m

    def share_forward(m):
        m["z"].wait_recv()
        other = m["lo"].at[y, 1 - zl, c]
        m["y"].append(Group([(other, other, p) for _, p in y_peers], m["lo"].at[0:3, 0, 0]))

    def share_across(m):
        for cp in m["yh"]:
            cp.wait_recv()
        column = m["hi"].at[:, zl, c]
        m["y"].append(send(column, column, z_peer))

    def share_core(m):
        for cp in m["y"]:
            cp.wait_recv()
        half = m["full"].at[:, :, c]
        m["c"] = send(half, half, c_peer)

    def share_wait(m):
        m["c"].wait_recv()

    e_x, e_z, merged_at, cots_at = ([None] * n for _ in range(4))

    def expert_part(k):
        start, size = chunks[k]
        b = per_chunk[k]
        for i, dx in enumerate(SHIFTS + (0,)):
            for z in range(2):
                to = z * NX + (x + dx) % NX
                total = jnp.zeros((rows, size), F32)
                for e in range(n_exp):
                    total += coef[to, sys_id * n_exp + e] * experts[e, :, start : start + size].astype(F32)
                b["epart"][i, z] = total.astype(BF16)
        if k == 0:
            e_z[0] = send_all(
                lambda dz, dx: b["epart"].at[(SHIFTS + (0,)).index(dx), (zh + dz) % 2], b["ez"], sys_peers
            )
        else:
            e_x[k] = send_all(lambda dx: b["epart"].at[SHIFTS.index(dx)], b["erecv"], x_peers)

    def expert_x(k):
        b = per_chunk[k]
        for cp in e_x[k]:
            cp.wait_recv()
        total = b["epart"][3].astype(F32)
        for i in range(3):
            total += b["erecv"][i].astype(F32)
        b["esum"][...] = total.astype(BF16)
        e_z[k] = [send(b["esum"].at[1 - zh], b["ez"].at[0], sys_peer(1, 0))]

    def merge(k):
        b = per_chunk[k]
        for cp in e_z[k]:
            cp.wait_recv()
        own = b["epart"].at[3] if k == 0 else b["esum"]
        total = own[pl.ds(zh, 1)][0].astype(F32)
        for i in range(b["ez"].shape[0]):
            total += b["ez"][i].astype(F32)
        b["merged"][pl.ds(y, 1), pl.ds(zl, 1), pl.ds(c, 1)] = total.astype(BF16)[None, None, None]
        merged_at[k] = share(b["merged"], rows * 3 // 7 if k == 0 else rows)
        if k > 1:
            cots_at[k] = share(b["cots"], own_atoms)

    def merge_forward(k):
        if k == 1:
            share_forward(cots_at[k])
        share_forward(merged_at[k])
        if k > 1:
            share_forward(cots_at[k])

    def merge_core(k):
        share_core(merged_at[k])

    def cots_core(k):
        share_core(cots_at[k])

    def merge_wait(k):
        share_wait(merged_at[k])

    def cots_wait(k):
        share_wait(cots_at[k])

    def one_hots():
        lane = lax.broadcasted_iota(jnp.int32, (128, 128), 1)

        def by_edge(j, _):
            at = pl.ds(pl.multiple_of(j * 128, 128), 128)
            for idx, out in ((src_rows, oh_src), (tgt_rows, oh_tgt)):
                col = jnp.broadcast_to(idx[pl.ds(j, 1), :], (128, 128)).T
                for a in range(n_atoms // 128):
                    out[at, a * 128 : (a + 1) * 128] = jnp.where(col == lane + a * 128, 1.0, 0.0).astype(BF16)
            return 0

        lax.fori_loop(0, n_edges // 128, by_edge, 0)
        sub = lax.broadcasted_iota(jnp.int32, (64, n_edges), 0)

        def by_atom(j, _):
            at = pl.ds(pl.multiple_of(j * 64, 64), 64)
            for idx, out in ((src_line, ot_src), (tgt_line, ot_tgt)):
                line = jnp.broadcast_to(idx[...], (64, n_edges)) - j * 64
                out[at, :] = jnp.where(line == sub, 1.0, 0.0).astype(BF16)
            return 0

        lax.fori_loop(0, n_atoms // 64, by_atom, 0)

    def select_atoms():
        count = 4 * rows
        i = lax.broadcasted_iota(jnp.int32, (count, width), 0)
        j = lax.broadcasted_iota(jnp.int32, (count, width), 1)
        pick = jnp.where(j == i + (i // rows + c) * rows, 1.0, 0.0).astype(BF16)
        sel_atoms[...] = dot_t(pick, at_all[...].reshape(n_atoms, width)).astype(BF16)

    p_c = [None] * n

    def projected(k):
        return per_chunk[k if k >= 2 else n - 1]["proj"]

    def project(k):
        size = chunks[k][1]
        b = per_chunk[k]
        out = projected(k)
        narrow = 2 * size <= out.shape[2]
        first, count = (2 * c, 2) if k >= 2 else (0, NY)

        def body(i, _):
            t = first + i
            at = pl.ds(pl.multiple_of(t * 256, 256), 256)
            a = at_all[pl.ds(t, 1)].reshape(256, width)
            w = [b["merged"][2 * h : 2 * h + 2].reshape(width, size) for h in range(2)]
            if narrow:
                both = dot(a, jnp.concatenate(w, axis=1)).astype(BF16)
                out[0, at, 0:size] = both[:, 0:size]
                out[1, at, 0:size] = both[:, size : 2 * size]
            else:
                for h in range(2):
                    out[h, at, 0:size] = dot(a, w[h]).astype(BF16)
            return 0

        lax.fori_loop(0, count, body, 0)
        if k >= 2:
            own = out.at[:, pl.ds(pl.multiple_of(c * (n_atoms // 2), 512), n_atoms // 2), 0:size]
            p_c[k] = send(own, own, c_peer)
        if narrow:
            out[1, :, size : 2 * size] = b["cots"][...].reshape(n_atoms, size)

    def project_wait(k):
        p_c[k].wait_recv()

    def pick_first():
        size = chunks[0][1]
        b = per_chunk[0]

        def body(t, _):
            at = pl.ds(pl.multiple_of(t * 512, 512), 512)
            edge_cots[t // 2, pl.ds(pl.multiple_of((t % 2) * 512, 512), 512), :] = dot(
                oh_tgt[at, :], b["cots"][...].reshape(n_atoms, size)
            ).astype(BF16)
            return 0

        lax.fori_loop(0, n_edges // 512, body, 0)

    def pick(k, half):
        start, size = chunks[k]
        b = per_chunk[k]
        pr = projected(k)
        narrow = 2 * size <= pr.shape[2]
        count = n_edges // 1024

        def body(t, _):
            at = pl.ds(pl.multiple_of(t * 512, 512), 512)
            o_s, o_t = oh_src[at, :], oh_tgt[at, :]
            if narrow:
                by_tgt = dot(o_t, pr[1, :, 0 : 2 * size])
                edge_cot = by_tgt[:, size : 2 * size]
                pre = dot(o_s, pr[0, :, 0:size]) + by_tgt[:, 0:size]
            else:
                pre = dot(o_s, pr[0, :, 0:size]) + dot(o_t, pr[1, :, 0:size])
                if k == 0:
                    edge_cot = edge_cots[t // 2, pl.ds(pl.multiple_of((t % 2) * 512, 512), 512), :].astype(F32)
                else:
                    edge_cot = dot(o_t, b["cots"][...].reshape(n_atoms, size))
            r = radial[at, start : start + size].astype(F32)
            g = 1.0 / (1.0 + jnp.exp(-pre))
            edge_vals[at, 0:size] = (edge_cot * r * (g * (1.0 + pre * (1.0 - g)))).astype(BF16)
            edge_vals[at, size : 2 * size] = (pre * g * r).astype(BF16)
            return 0

        lax.fori_loop(half * count, (half + 1) * count, body, 0)

    c_recv = [None] * n

    def sums(k, tiles):
        size = chunks[k][1]
        b = per_chunk[k]
        if c_recv[k] is None:
            c_recv[k] = []
        for d in tiles:
            pair = (y // 2 + d) % 2
            at = pl.ds(pl.multiple_of(pair * (n_atoms // 2), n_atoms // 2), n_atoms // 2)
            o_s, o_t = ot_src[at, :], ot_tgt[at, :]
            by_src = dot(o_s, edge_vals[:, 0:size]).astype(BF16)
            by_tgt = dot(o_t, edge_vals[:, 0 : 2 * size]).astype(BF16)
            spot = pl.ds(pair * 2, 2)
            b["sums"][spot, :, :, :, 0:size] = by_src.reshape(2, 2, 2, own_atoms, size)
            b["sums"][spot, :, :, :, size : 3 * size] = by_tgt.reshape(2, 2, 2, own_atoms, 2 * size)
            c_recv[k].append((pair, send(b["sums"].at[spot], b["csums"].at[spot], c_peer)))

    w_z, w_y, g_z, g_y, n_y, n_z, d_z, d_x = ([None] * n for _ in range(8))

    h_y = []

    def atoms_of(dy, dz):
        return (y + dy) % NY, (zl + dz) % 2

    def reduce_core(k):
        size = chunks[k][1]
        b = per_chunk[k]
        for pair, cp in c_recv[k]:
            cp.wait_recv()
            spot = pl.ds(pair * 2, 2)
            both = b["sums"][spot, :, :, :, 0 : 2 * size].astype(F32) + b["csums"][spot, :, :, :, 0 : 2 * size].astype(F32)
            b["chip"][spot] = both.astype(BF16)
        grad = dot(sel_atoms[...], b["chip"][...].reshape(n_atoms, 2 * size)).astype(BF16)
        b["wpart"][0:2] = grad[:, 0:size].reshape(2, 2, rows, size)
        b["wpart"][2:4] = grad[:, size : 2 * size].reshape(2, 2, rows, size)
        if k > 0:
            w_y[k] = send_all(lambda dy, dz: b["wpart"].at[atoms_of(dy, dz)], b["wd"], edge_peers)
        else:
            w_z[k] = send(b["wpart"].at[:, 1 - zl], b["wz"], z_peer)

    def node_core(k):
        size = chunks[k][1]
        b = per_chunk[k]
        spot = (slice(None), slice(None), pl.ds(c, 1), slice(None), slice(2 * size, 3 * size))
        both = b["sums"][spot].astype(F32) + b["csums"][spot].astype(F32)
        b["nchip"][...] = both.astype(BF16).reshape(NY, 2, own_atoms, size)
        n_y[k] = send_all(lambda d: b["nchip"].at[(y + d) % NY], b["ny"], y_peers)

    def node_z(k):
        b = per_chunk[k]
        for cp in n_y[k]:
            cp.wait_recv()
        total = b["nchip"][pl.ds(y, 1)][0].astype(F32)
        for i in range(3):
            total += b["ny"][i].astype(F32)
        b["nsum"][...] = total.astype(BF16)
        n_z[k] = send(b["nsum"].at[1 - zl], b["nz"], z_peer)

    def node_finish(k):
        start, size = chunks[k]
        b = per_chunk[k]
        n_z[k].wait_recv()
        total = b["nsum"][pl.ds(zl, 1)][0].astype(F32) + b["nz"][...].astype(F32)
        node_out[:, start : start + size] = total.astype(BF16)

    def zy_part(k):
        return chunks[k][1] * (1 if k == 2 else 2)

    def atom_send(k):
        b = per_chunk[k]
        part = zy_part(k)
        if k == 3:
            g_y[k] = send_all(lambda dy, dz: b["chip"].at[(*atoms_of(dy, dz), c)], b["gd"], edge_peers)
            return
        g_z[k] = send(b["chip"].at[:, 1 - zl, c, :, 0:part], b["gz"], z_peer)
        if k == 2:
            h_y.extend(send_all(lambda d: b["chip"].at[(y + d) % NY, :, c, :, part : 2 * part], b["hd"], y_peers))

    def atom_forward(k):
        part = zy_part(k)
        b = per_chunk[k]
        g_z[k].wait_recv()
        own = b["chip"][:, pl.ds(zl, 1), pl.ds(c, 1), :, 0:part].reshape(NY, own_atoms, part)
        b["gsum"][...] = (own.astype(F32) + b["gz"][...].astype(F32)).astype(BF16)
        g_y[k] = send_all(lambda d: b["gsum"].at[(y + d) % NY], b["gd"], y_peers)

    def atom_across(k):
        part = zy_part(k)
        b = per_chunk[k]
        h_y[0].wait_recv()
        total = b["chip"][pl.ds(y, 1), :, pl.ds(c, 1), :, part : 2 * part].reshape(2, own_atoms, part).astype(F32)
        for i in range(3):
            total += b["hd"][i].astype(F32)
        b["hsum"][...] = total.astype(BF16)
        h_y.append(send(b["hsum"].at[1 - zl], b["hz"], z_peer))

    def atom_finish(k):
        size = chunks[k][1]
        b = per_chunk[k]
        g_y[k][0].wait_recv()
        if k < 3:
            total = b["gsum"][pl.ds(y, 1)][0].astype(F32)
        else:
            total = b["chip"][pl.ds(y, 1), pl.ds(zl, 1), pl.ds(c, 1)][0, 0, 0].astype(F32)
        for i in range(b["gd"].shape[0]):
            total += b["gd"][i].astype(F32)
        if k == 2:
            h_y[1].wait_recv()
            rest = b["hsum"][pl.ds(zl, 1)][0].astype(F32) + b["hz"][...].astype(F32)
            total = jnp.concatenate([total, rest], axis=1)
        g = total.astype(BF16)
        grad = dot_t(g[:, 0:size], b["merged"][0:2].reshape(width, size))
        grad += dot_t(g[:, size : 2 * size], b["merged"][2:4].reshape(width, size))
        if k == 0:
            atom_grad[...] = grad
        else:
            atom_grad[...] += grad

    def weight_z(k):
        size = chunks[k][1]
        b = per_chunk[k]
        w_z[k].wait_recv()
        own = b["wpart"][:, pl.ds(zl, 1)].reshape(NY, rows, size)
        b["wsum"][...] = (own.astype(F32) + b["wz"][...].astype(F32)).astype(BF16)
        w_y[k] = send_all(lambda d: b["wsum"].at[(y + d) % NY], b["wd"], y_peers)

    def weight_finish(k):
        b = per_chunk[k]
        for cp in w_y[k]:
            cp.wait_recv()
        if k > 0:
            total = b["wpart"][pl.ds(y, 1), pl.ds(zl, 1)][0].astype(F32)
        else:
            total = b["wsum"][pl.ds(y, 1)].astype(F32)
        for i in range(b["wd"].shape[0]):
            total += b["wd"][i : i + 1].astype(F32)
        b["dall"][pl.ds(sys_id, 1)] = total.astype(BF16)
        own = b["dall"].at[sys_id]
        if k == n - 1:
            d_x[k] = [Group([(own, own, p) for _, p in sys_peers], b["dall"].at[0:7])]
        else:
            d_z[k] = send(own, own, sys_peer(1, 0))
            d_x[k] = [Group([(own, own, p) for _, p in x_peers], b["dall"].at[0:3])]

    def expert_forward(k):
        d_z[k].wait_recv()
        other = per_chunk[k]["dall"].at[(1 - zh) * NX + x]
        d_x[k].append(Group([(other, other, p) for _, p in x_peers], per_chunk[k]["dall"].at[0:3]))

    def expert_finish(k):
        start, size = chunks[k]
        b = per_chunk[k]
        for cp in d_x[k]:
            cp.wait_recv()
        for e in range(n_exp):
            total = jnp.zeros((rows, size), F32)
            for s in range(2 * NX):
                total += coef[s, sys_id * n_exp + e] * b["dall"][s].astype(F32)
            expert_grad[e, :, start : start + size] = total
        cols = slice(start, start + size)
        outputs.append(fetch(expert_grad.at[:, :, cols], expert_hbm.at[:, :, cols]))

    outputs = []
    atoms_in.wait()
    atoms_at = share(at_all, own_atoms // 2)
    for cp in cot_in:
        cp.wait()
    cots_at[0] = share(per_chunk[0]["cots"], own_atoms // 2)
    coef_in.wait()
    experts_in.wait()
    for k in range(n):
        expert_part(k)
    for cp in index_in:
        cp.wait()
    one_hots()
    share_forward(atoms_at)
    share_forward(cots_at[0])
    share_across(atoms_at)
    share_across(cots_at[0])
    merge(0)
    share_forward(merged_at[0])
    expert_x(1)
    share_core(atoms_at)
    share_across(merged_at[0])
    share_core(cots_at[0])
    share_wait(atoms_at)
    select_atoms()
    cots_at[1] = share(per_chunk[1]["cots"], own_atoms)
    cots_wait(0)
    pick_first()
    share_core(merged_at[0])
    radial_in.wait()
    merge(1)
    merge_wait(0)

    work = (
        lambda k: project_wait(k) if k >= 2 else project(k),
        lambda k: pick(k, 0),
        lambda k: pick(k, 1),
        lambda k: sums(k, (1,)),
        lambda k: sums(k, (0,)),
    )
    beside = {
        (0, 0): ((merge_forward, 1), (expert_x, 2)),
        (0, 2): ((expert_x, 3),),
        (0, 3): ((merge, 2), (merge_core, 1)),
        (0, 4): ((cots_core, 1), (merge_wait, 1)),
        (1, 0): ((merge_forward, 2), (merge, 3), (reduce_core, 0), (node_core, 0), (atom_send, 0), (cots_wait, 1)),
        (1, 1): ((merge_forward, 3),),
        (1, 2): ((merge_core, 2),),
        (1, 3): ((merge_wait, 2), (project, 2), (cots_core, 2)),
        (1, 4): ((weight_z, 0),),
        (2, 0): ((cots_wait, 2),),
        (2, 1): ((reduce_core, 1), (node_core, 1), (atom_send, 1), (atom_forward, 0)),
        (2, 2): ((merge_core, 3), (cots_core, 3), (weight_finish, 0)),
        (2, 3): ((merge_wait, 3), (cots_wait, 3), (project, 3), (node_z, 0)),
        (3, 1): ((reduce_core, 2), (atom_send, 2)),
        (3, 2): ((weight_finish, 1),),
        (3, 3): ((node_z, 1),),
    }
    for k in range(n):
        for slot, f in enumerate(work):
            f(k)
            for g, i in beside.get((k, slot), ()):
                g(i)
    reduce_core(3)
    atom_forward(1)
    node_core(2)
    node_core(3)
    expert_forward(0)
    weight_finish(2)
    atom_send(3)
    expert_forward(1)
    atom_across(2)
    atom_finish(0)
    expert_finish(0)
    atom_forward(2)
    weight_finish(3)
    expert_forward(2)
    atom_finish(1)
    node_z(2)
    expert_finish(1)
    node_z(3)
    atom_finish(2)
    for k in range(n):
        node_finish(k)
    outputs.append(fetch(node_out, node_hbm))
    atom_finish(3)
    outputs.append(fetch(atom_grad, atom_hbm))
    expert_finish(2)
    expert_finish(3)

    def finish():
        for cp in outputs:
            cp.wait()

    def drain():
        for cp in sent[-SEND_SLOTS:]:
            cp.wait_send()
        assert len(groups) == recv_sem.shape[0], len(groups)

    finish()
    drain()


def write_out(*refs):
    count = (len(refs) - 1) // 3
    sem = refs[-1]
    moves = []
    for src, dst, buf in zip(refs[:count], refs[count : 2 * count], refs[2 * count : 3 * count]):
        for i in range(src.shape[0]):
            moves.append((src.at[i], buf.at[i], dst.at[i]))
    reads = [pltpu.make_async_copy(s, b, sem.at[0, i]) for i, (s, b, _) in enumerate(moves)]
    writes = [pltpu.make_async_copy(b, d, sem.at[1, i]) for i, (_, b, d) in enumerate(moves)]
    for r in reads:
        r.start()
    for r, w in zip(reads, writes):
        r.wait()
        w.start()
    for w in writes:
        w.wait()


def layer(atoms, cotangent, experts, radial, coef, source, target):
    n_exp, rows, width = experts.shape
    own = atoms.shape[1]
    n_atoms = 16 * own
    n_edges = radial.shape[1]
    chunks, at = [], 0
    while at < width:
        size = min(256, width - at)
        chunks.append((at, size))
        at += size

    def vmem(*shape):
        return pltpu.VMEM(shape, BF16)

    def vmem_if(used, *shape):
        return vmem(*shape) if used else vmem(16, 128)

    per_chunk = [
        {
            "epart": vmem(4, 2, rows, s),
            "erecv": vmem_if(k > 0, 3, 2, rows, s),
            "esum": vmem_if(k > 0, 2, rows, s),
            "ez": vmem(7 if k == 0 else 1, rows, s),
            "cots": vmem(NY, 2, 2, own, s),
            "merged": vmem(NY, 2, 2, rows, s),
            "sums": vmem(NY, 2, 2, own, 3 * s),
            "csums": vmem(NY, 2, 2, own, 3 * s),
            "chip": vmem(NY, 2, 2, own, 2 * s),
            "nchip": vmem(NY, 2, own, s),
            "ny": vmem(3, 2, own, s),
            "nsum": vmem(2, own, s),
            "nz": vmem(own, s),
            "gz": vmem_if(k < 3, NY, own, s if k == 2 else 2 * s),
            "gsum": vmem_if(k < 3, NY, own, s if k == 2 else 2 * s),
            "gd": vmem(3 if k < 3 else 7, own, s if k == 2 else 2 * s),
            "hd": vmem_if(k == 2, 3, 2, own, s),
            "hsum": vmem_if(k == 2, 2, own, s),
            "hz": vmem_if(k == 2, own, s),
            "wpart": vmem(NY, 2, rows, s),
            "wz": vmem_if(k == 0, NY, rows, s),
            "wsum": vmem_if(k == 0, NY, rows, s),
            "wd": vmem(7 if k > 0 else 3, rows, s),
            "dall": vmem(8, rows, s),
            "proj": vmem_if(k >= 2, 2, n_atoms, 256),
        }
        for k, (_, s) in enumerate(chunks)
    ]
    wide = max(s for _, s in chunks)
    hbm = pl.BlockSpec(memory_space=pl.ANY)
    node, agrad, egrad = pl.pallas_call(
        functools.partial(kernel, chunks),
        out_shape=(
            jax.ShapeDtypeStruct((own, width), BF16),
            jax.ShapeDtypeStruct((own, width), F32),
            jax.ShapeDtypeStruct((n_exp, rows, width), F32),
        ),
        in_specs=[hbm] * 9,
        out_specs=(hbm, hbm, hbm),
        scratch_shapes=[
            vmem(own, width),
            pltpu.VMEM((own, width), F32),
            pltpu.VMEM((n_exp, rows, width), F32),
            pltpu.SMEM(coef.shape, F32),
            pltpu.VMEM((n_edges // 128, 128), jnp.int32),
            pltpu.VMEM((n_edges // 128, 128), jnp.int32),
            pltpu.VMEM((1, n_edges), jnp.int32),
            pltpu.VMEM((1, n_edges), jnp.int32),
            vmem(n_exp, rows, width),
            vmem(n_edges, width),
            vmem(NY, 2, 2, own, width),
            vmem(n_edges, n_atoms),
            vmem(n_edges, n_atoms),
            vmem(n_atoms, n_edges),
            vmem(n_atoms, n_edges),
            vmem(4 * rows, n_atoms),
            vmem(n_edges, 2 * wide),
            per_chunk,
            pltpu.SemaphoreType.DMA((10 + 2 * len(chunks),)),
            pltpu.SemaphoreType.DMA((SEND_SLOTS,)),
            pltpu.SemaphoreType.DMA((RECV_SLOTS,)),
        ],
        compiler_params=pltpu.CompilerParams(
            collective_id=0, has_side_effects=True, vmem_limit_bytes=67043328
        ),
    )(
        experts,
        coef,
        atoms[0],
        cotangent[0],
        radial[0],
        source.reshape(n_edges // 128, 128),
        target.reshape(n_edges // 128, 128),
        source,
        target,
    )
    results = (node[None], agrad[None], egrad)
    moves = sum(r.shape[0] for r in results)
    return pl.pallas_call(
        write_out,
        out_shape=tuple(jax.ShapeDtypeStruct(r.shape, r.dtype) for r in results),
        in_specs=[hbm] * 3,
        out_specs=(hbm,) * 3,
        scratch_shapes=[pltpu.VMEM(r.shape, r.dtype) for r in results] + [pltpu.SemaphoreType.DMA((2, moves))],
    )(*results)


def solution(mesh):
    spec = P("sys", "edge", None)
    return jax.shard_map(
        layer,
        mesh=mesh,
        in_specs=(spec, spec, spec, spec, P(), P("sys", "edge"), P("sys", "edge")),
        out_specs=(spec, spec, spec),
        check_vma=False,
    )
```
